256 devices in a mesh: tmpl: 32 (over z, x), tm: 8 (over y, core).
Axes of the slice: x: 4, y: 4, z: 8, core: 2. Of those that a mesh axis runs over, the one named last changes fastest.
Arguments:
- traces: bfloat16 [2048, 3, 16384], P('tmpl', None, 'tm'), may hold values from -1000 to 1000
- group_stations: int32 [32, 32], replicated, may hold values from 0 to 2047, as said below
- template_stations: int32 [1024, 8], P('tmpl'), may hold values from 0 to 2047, as said below
- templates: bfloat16 [1024, 9600], P(('tmpl', 'tm')), may hold values from -6 to 6
Outputs:
- detection: bfloat16 [1024, 16384], P('tmpl', 'tm')
The draws below stay inside these ranges and needn't reach their ends.
Inputs may be any that keep to these rules, and one draw needn't show every extreme that they name: `group_stations`: row g lists 32 distinct station ids in ascending order. Station i's traces lie on index i // 64 of tmpl; at most 2 ids of a row share such an index, and every row has an index with exactly 2. `template_stations`: row k lists 8 distinct ids, all from row k // 32 of group_stations; every id of that row appears in some template of the group.
All inputs are finite; a program needn't handle non-finite values.
Results may differ from the reference program's by a relative error of at most 0.0049.
Values may be sent and summed in bfloat16 or wider, within the bound.
A program may use at most 64 MiB of HBM per device.

```python
import math
import jax
import jax.numpy as jnp
from jax import lax

CHANS = 3
SLOTS = 8
TLEN = 400
S_GRP = 32
STA_DEV = 64
TPL_GRP = 32
GROUPS = 32
STATIONS = 2048
TEMPLATES = 1024
SAMPLES = 16384
CAP = 2


def group_list(group_key):
    first_key, other_key, row_key = jax.random.split(group_key, 3)
    first_home = jax.random.randint(first_key, (), 0, GROUPS).astype(jnp.int32)
    others = jax.random.permutation(other_key, (GROUPS - 1) * CAP)[:S_GRP - CAP].astype(jnp.int32)
    other_home = others // CAP
    other_home = other_home + (other_home >= first_home).astype(jnp.int32)
    home_ids = jnp.concatenate([jnp.full((CAP,), first_home, jnp.int32), other_home])
    rank_ids = jnp.concatenate([jnp.arange(CAP, dtype=jnp.int32), others % CAP])
    row_keys = jax.random.split(row_key, GROUPS)
    row_table = jax.vmap(lambda one_key: jax.random.permutation(one_key, STA_DEV)[:CAP])(row_keys).astype(jnp.int32)
    return jnp.sort(home_ids * STA_DEV + row_table[home_ids, rank_ids])


def station_tables(key):
    base_key = jax.random.fold_in(key, 11)
    group_keys = jax.random.split(jax.random.fold_in(base_key, 1), GROUPS)
    members = jax.vmap(group_list)(group_keys)
    template_keys = jax.random.split(jax.random.fold_in(base_key, 2), TEMPLATES)
    leading = jnp.arange(TEMPLATES, dtype=jnp.int32) % S_GRP
    shifts = jax.vmap(lambda one_key: jax.random.permutation(one_key, S_GRP - 1)[:SLOTS - 1])(template_keys).astype(jnp.int32)
    picked = jnp.concatenate([leading[:, None], (leading[:, None] + 1 + shifts) % S_GRP], axis=1)
    owner_group = jnp.arange(TEMPLATES, dtype=jnp.int32) // TPL_GRP
    return (members, members[owner_group[:, None], picked])


def draw_group_stations(key, part):
    return station_tables(key)[0]


def draw_template_stations(key, part):
    return station_tables(key)[1]


def draw_traces(key, part):
    random_key, scale_key = jax.random.split(jax.random.fold_in(key, 3))
    time_frac = jnp.arange(SAMPLES, dtype=jnp.float32) / SAMPLES
    scales = jnp.exp(jax.random.uniform(scale_key, (STATIONS, CHANS, 1), jnp.float32, 0.0, math.log(10.0)))
    random_part = jnp.clip(jax.random.normal(random_key, (STATIONS, CHANS, SAMPLES), jnp.float32), -6.0, 6.0)
    envelope = jnp.exp(math.log(10.0) * time_frac)
    return (scales * envelope * random_part).astype(jnp.bfloat16)


def block_scale(key, extent, cuts, least, high):
    loudness, own = 1.0, jax.random.fold_in(key, 6)
    for position, parts in cuts:
        draws = jnp.exp(jax.random.uniform(jax.random.fold_in(own, position), (parts,), jnp.float32, least / len(cuts), high / len(cuts)))
        loudness = loudness * jnp.repeat(draws, extent[position] // parts).reshape([-1 if axis == position else 1 for axis in range(len(extent))])
    return loudness


def centred(own_key, shape, scale, reach, shards=(), kind=jnp.bfloat16):
    values = jax.random.normal(own_key, shape, jnp.float32) * scale
    if len(shards) > 0:
        values = block_scale(own_key, shape, shards, -0.22, 0.18) * values
    return jnp.clip(values, min=-reach, max=reach).astype(kind)


def setup_inputs(seed: int = 0) -> dict:
    arg_keys = jax.random.split(jax.random.key(seed), 5)
    traces = draw_traces(jax.random.fold_in(arg_keys[4], 71), 0)
    group_stations = draw_group_stations(jax.random.fold_in(arg_keys[4], 71), 0)
    template_stations = draw_template_stations(jax.random.fold_in(arg_keys[4], 71), 0)
    templates = centred(arg_keys[3], (TEMPLATES, SLOTS * CHANS * TLEN), 1.0, 6.0, ((0, 256),))
    return {"traces": traces, "group_stations": group_stations, "template_stations": template_stations, "templates": templates}


def dense_kernel(panel, station_lists, members):
    count = panel.shape[0]
    onehot = (station_lists[:, :, None] == members[None, None, :]).astype(jnp.float32)
    shaped = panel.astype(jnp.float32).reshape(count, SLOTS, CHANS * TLEN)
    dense = jnp.einsum('nsj,nsq->njq', onehot, shaped, precision=lax.Precision.HIGHEST)
    dense = lax.optimization_barrier(dense.astype(jnp.bfloat16))
    return dense.reshape(count, S_GRP * CHANS, TLEN)

def correlate(window, kernel):
    result = lax.conv_general_dilated(window.astype(jnp.float32)[None], kernel.astype(jnp.float32), (1,), 'VALID', dimension_numbers=('NCH', 'OIH', 'NCH'), precision=lax.Precision.HIGHEST)
    return result[0]

def reference(traces, group_stations, template_stations, templates):
    wide = traces.astype(jnp.float32)
    power = lax.optimization_barrier(jnp.sum(wide * wide, axis=2))
    spread = jnp.sqrt(power / SAMPLES + 1e-06)
    scaled = lax.optimization_barrier((wide / spread[:, :, None]).astype(jnp.bfloat16))
    padded = jnp.pad(scaled, ((0, 0), (0, 0), (0, TLEN - 1)))
    lists = template_stations.reshape(GROUPS, TPL_GRP, SLOTS)
    panels = templates.reshape(GROUPS, TPL_GRP, SLOTS * CHANS * TLEN)

    def one_group(inputs):
        members, station_lists, panel = inputs
        window = padded[members].reshape(S_GRP * CHANS, SAMPLES + TLEN - 1)
        stacked = correlate(window, dense_kernel(panel, station_lists, members))
        level = jnp.sqrt(lax.optimization_barrier(jnp.sum(stacked * stacked, axis=1)) / SAMPLES + 1e-06)
        return (stacked / level[:, None]).astype(jnp.bfloat16)
    detection = lax.map(one_group, (group_stations, lists, panels))
    return detection.reshape(TEMPLATES, SAMPLES)
```

```python
import jax
import jax.numpy as jnp
from jax import lax
from jax.experimental import pallas as pl
from jax.experimental.pallas import tpu as pltpu
from jax.sharding import PartitionSpec as P

BF = jnp.bfloat16
F32 = jnp.float32
KQ = 1664


def lroll(x, s):
    s %= 128
    return x if s == 0 else pltpu.roll(x, s, 1)


def build_w(mem_ref, ts_ref, t_ref, w_ref):
    lane = lax.broadcasted_iota(jnp.int32, (32, 128), 1)

    def step(jq, _):
        tails = [None] * 3
        for g in range(4):
            m = mem_ref[jq * 4 + g]
            oh = [jnp.where(ts_ref[s] == m, 1.0, 0.0).astype(BF) for s in range(8)]
            for c in range(3):
                kern = []
                for t in range(4):
                    a = oh[0] * t_ref[c, :, t * 128 : (t + 1) * 128]
                    for s in range(1, 8):
                        a = a + oh[s] * t_ref[s * 3 + c, :, t * 128 : (t + 1) * 128]
                    kern.append(a)
                tl = lroll(kern[3], 32 * g)
                tails[c] = tl if g == 0 else tails[c] + tl
                q = c * 8 + jq
                for r in range(8):
                    rl = [lroll(kern[t], r) for t in range(3)]
                    for t in range(3):
                        v = rl[t]
                        if r:
                            v = jnp.where(lane < r, rl[t - 1] if t else jnp.zeros_like(v), v)
                        lo = g * 384 + t * 128
                        w_ref[q, r * 32 : r * 32 + 32, lo : lo + 128] = v
        for c in range(3):
            for r in range(8):
                v = lroll(tails[c], -(8 - r))
                v = jnp.where((lane & 31) < 24, v, jnp.zeros_like(v))
                w_ref[c * 8 + jq, r * 32 : r * 32 + 32, 1536:1664] = v
        return 0

    lax.fori_loop(0, 8, step, 0)


def build_a(slot_ref, inv_ref, x_ref, xs_ref, a_ref, c, jq):
    lane = lax.broadcasted_iota(jnp.int32, (16, 128), 1)
    tails = [None] * 16
    for g in range(4):
        slot = slot_ref[jq * 4 + g]
        xs_ref[g, 0:20, :] = x_ref[slot, c].astype(F32) * inv_ref[slot, c]
        xm = [xs_ref[g, m : m + 16, :].astype(BF) for m in range(5)]
        for p in range(16):
            rl = [lroll(xm[m], -8 * p) for m in range(4)]
            for m in range(3):
                v = rl[m] if p == 0 else jnp.where(lane < 128 - 8 * p, rl[m], rl[m + 1])
                lo = g * 384 + m * 128
                a_ref[p * 16 : p * 16 + 16, lo : lo + 128] = v
            tl = rl[3]
            if p >= 14:
                tl = jnp.where(lane < 128 - 8 * p, tl, lroll(xm[4], -8 * p))
            tl = lroll(tl, 32 * g)
            tails[p] = tl if g == 0 else jnp.where(lane < 32 * g, tails[p], tl)
    for p in range(16):
        a_ref[p * 16 : p * 16 + 16, 1536:1664] = tails[p]


def corr_kernel(mem_ref, slot_ref, inv_ref, ts_ref, t_ref, x_ref, o_ref, w_ref, a_ref, xs_ref):
    build_w(mem_ref, ts_ref, t_ref, w_ref)
    o_ref[...] = jnp.zeros_like(o_ref)

    def step(q, _):
        build_a(slot_ref, inv_ref, x_ref, xs_ref, a_ref, q // 8, q % 8)
        o_ref[...] += lax.dot_general(
            a_ref[...], w_ref[q], (((1,), (1,)), ((), ())), preferred_element_type=F32
        )
        return 0

    lax.fori_loop(0, 24, step, 0)


def correlate(members, slots, inv, ts, t, x):
    smem = pl.BlockSpec(memory_space=pltpu.SMEM)
    vmem = pl.BlockSpec(memory_space=pltpu.VMEM)
    return pl.pallas_call(
        corr_kernel,
        out_shape=jax.ShapeDtypeStruct((256, 256), F32),
        in_specs=[smem, smem, smem, vmem, vmem, vmem],
        out_specs=vmem,
        scratch_shapes=[
            pltpu.VMEM((24, 256, KQ), BF),
            pltpu.VMEM((256, KQ), BF),
            pltpu.VMEM((4, 24, 128), F32),
        ],
        compiler_params=pltpu.CompilerParams(vmem_limit_bytes=56 << 20),
    )(members, slots, inv, ts, t, x)


def body(traces, group_stations, template_stations, templates):
    sta_dev, chans, stretch = traces.shape
    groups = lax.axis_size("tmpl")
    parts = lax.axis_size("tm")
    me = lax.axis_index("tmpl")
    s_grp = group_stations.shape[1]
    samples = stretch * parts
    local = group_stations - me * sta_dev
    mine = (local >= 0) & (local < sta_dev)
    second = mine & jnp.pad(mine, ((0, 0), (1, 0)))[:, :-1]
    first = mine & ~second
    ids = jnp.stack([jnp.max(jnp.where(f, local, -1), axis=1) for f in (first, second)], axis=1)
    pick = (ids[:, :, None] == jnp.arange(sta_dev)[None, None, :]).astype(BF)
    outgoing = jnp.einsum("gir,rct->gict", pick, traces, preferred_element_type=F32).astype(BF)
    x = lax.all_to_all(outgoing, "tmpl", split_axis=0, concat_axis=0, tiled=True)
    x = x.reshape(2 * groups, chans, stretch)
    members = group_stations[me]
    home = members // sta_dev
    rank = jnp.pad((home[1:] == home[:-1]).astype(jnp.int32), (1, 0))
    slots = home * 2 + rank
    power = lax.psum(jnp.sum(jnp.square(x.astype(F32)), axis=2), "tm")
    inv = 1.0 / jnp.sqrt(power / samples + 1e-06)
    rim = lax.ppermute(x[:, :, :512], "tm", [(i + 1, i) for i in range(parts - 1)])
    window = jnp.concatenate([x, rim], axis=2).reshape(2 * groups, chans, 20, 128)
    t = lax.all_gather(templates, "tm", axis=0, tiled=True).reshape(32, 24, 400)
    t = jnp.pad(t, ((0, 0), (0, 0), (0, 8)))
    tail = jnp.pad(t[:, :, 376:400], ((0, 0), (0, 0), (0, 104)))
    t = jnp.concatenate([t[:, :, :384], tail], axis=2).transpose(1, 0, 2)
    ts = jnp.broadcast_to(template_stations.T[:, :, None], (8, 32, 128))
    o = correlate(members, slots, inv, ts, t, window)
    stacked = o.reshape(16, 16, 8, 32).transpose(3, 1, 0, 2).reshape(32, stretch)
    level = lax.psum(jnp.sum(stacked * stacked, axis=1), "tm")
    return (stacked / jnp.sqrt(level / samples + 1e-06)[:, None]).astype(BF)


def solution(mesh):
    placed = (P("tmpl", None, "tm"), P(), P("tmpl", None), P(("tmpl", "tm"), None))
    return jax.shard_map(
        body, mesh=mesh, in_specs=placed, out_specs=P("tmpl", "tm"), check_vma=False
    )
```

```python
import jax
import jax.numpy as jnp
from jax import lax
from jax.experimental import pallas as pl
from jax.experimental.pallas import tpu as pltpu
from jax.sharding import PartitionSpec as P

BF = jnp.bfloat16
F32 = jnp.float32
MESH = pl.DeviceIdType.MESH
HOMES, PARTS, STA, MEMBERS, TPL, CHANS = 32, 8, 64, 32, 32, 3
SAMPLES = 16384
NV = 51
NROW = 67 * 16
VU = 3
VD = 17


def lroll(x, s):
    s %= 128
    return x if s == 0 else pltpu.roll(x, s, 1)


def lane_bits(rows):
    lane = lax.broadcasted_iota(jnp.int32, (rows, 128), 1)
    return [((lane >> (3 + s)) & 1).astype(F32).astype(BF) > BF(0.5) for s in range(4)]


def swap_blocks(x, bits):
    x = list(x)
    for s in range(4):
        d = 1 << s
        y = list(x)
        for i in range(16):
            if i & d:
                continue
            a, b = x[i], x[i + d]
            y[i] = jnp.where(bits[s], lroll(b, 8 * d), a)
            y[i + d] = jnp.where(bits[s], b, lroll(a, -8 * d))
        x = y
    return x


def pick_kernel(gs_ref, tr_ref, tp_ref, send_ref, pw_ref, tl_ref, rows, pscr):
    me = lax.axis_index("tmpl")
    local = (gs_ref[...] - me * STA).astype(F32)
    mine = (local >= 0) & (local < STA)
    low = jnp.min(jnp.where(mine, local, 1e6), axis=1, keepdims=True)
    high = jnp.max(jnp.where(mine, local, -1.0), axis=1, keepdims=True)
    high = jnp.where(high > low, high, -2.0)
    row = lax.broadcasted_iota(jnp.int32, (HOMES, STA), 1).astype(F32)
    pick = jnp.concatenate([(row == low).astype(F32), (row == high).astype(F32)], axis=0).astype(BF)
    lane = lax.broadcasted_iota(jnp.int32, (HOMES, 128), 1)
    power = jnp.zeros((HOMES, 128), F32)
    for c in range(CHANS):
        sq = jnp.zeros((64, 128), F32)
        for ch in range(4):
            res = jnp.dot(
                pick, tr_ref[c, :, ch * 512 : ch * 512 + 512], preferred_element_type=F32
            )
            for n in range(4):
                v = res[:, n * 128 : n * 128 + 128]
                sq = sq + v * v
                rows[c, pl.ds(ch * 4 + n, 64, stride=16), :] = v
        tot = jnp.sum(sq, axis=1, keepdims=True)
        for i in range(2):
            power = jnp.where(lane == c * 2 + i, tot[i * 32 : i * 32 + 32], power)
    pscr[...] = power

    def pack(g, _):
        for i in range(2):
            for c in range(CHANS):
                v = rows[c, pl.ds(pl.multiple_of((i * 32 + g) * 16, 16), 16), :].astype(BF)
                send_ref[g, 0, i, c] = v[:8]
                send_ref[g, 1, i, c] = v[8:]
        pw_ref[g] = pscr[pl.ds(g, 1), :]
        return 0

    lax.fori_loop(0, HOMES, pack, 0, unroll=4)
    for n in range(24):
        t = tp_ref[:, n * 400 : n * 400 + 400]
        tl_ref[n] = jnp.concatenate([t, jnp.zeros((4, 112), BF)], axis=1)


def pick_rows(gs, traces, templates):
    vmem = pl.BlockSpec(memory_space=pltpu.VMEM)
    return pl.pallas_call(
        pick_kernel,
        out_shape=[
            jax.ShapeDtypeStruct((HOMES, 2, 2, CHANS, 8, 128), BF),
            jax.ShapeDtypeStruct((HOMES, 1, 128), F32),
            jax.ShapeDtypeStruct((24, 4, 512), BF),
        ],
        in_specs=[vmem] * 3,
        out_specs=[vmem] * 3,
        scratch_shapes=[pltpu.VMEM((CHANS, 1024, 128), F32), pltpu.VMEM((HOMES, 128), F32)],
        compiler_params=pltpu.CompilerParams(vmem_limit_bytes=32 << 20),
    )(gs, traces, templates)


def main_kernel(
    gs_ref, ts_ref, tl_ref, send_ref, pw_ref, o_ref,
    w_ref, w0_ref, p8_ref, e_ref, yf_ref, oh_ref, tsb_ref, tg_ref, tf_ref, t_ref,
    r0_ref, r1_ref, hs_ref, hr_ref, pa_ref, p2_ref, inv_ref, ls_ref, la_ref,
    tsend, trecv, psend, precv, xsend, xrecv, asend, arecv, hsend, hrecv, lsend, lrecv,
):
    me = lax.axis_index("tmpl")
    my = lax.axis_index("tm")
    rx = (r0_ref, r1_ref)

    def home(d):
        z = lax.rem(me // 4 + d // 4, 8)
        return z * 4 + lax.rem(me % 4 + d % 4, 4)

    def back(d):
        z = lax.rem(me // 4 + 8 - d // 4, 8)
        return z * 4 + lax.rem(me % 4 + 4 - d % 4, 4)

    def loop(n, f):
        def step(d, _):
            f(d)
            return 0

        lax.fori_loop(1, n, step, 0)

    def copy(src, dst, send, recv, to):
        return pltpu.make_async_remote_copy(
            src_ref=src, dst_ref=dst, send_sem=send, recv_sem=recv, device_id=to, device_id_type=MESH
        )

    def tcopy(d, slot):
        to = {"tm": lax.rem(my + d, PARTS)}
        return copy(tl_ref, tg_ref.at[slot], tsend.at[d], trecv.at[slot], to)

    def pcopy(d, slot):
        to = home(d)
        return copy(pw_ref.at[to], pa_ref.at[my, slot], psend.at[d], precv.at[slot], {"tmpl": to})

    def xcopy(d, part, slot):
        to = home(d)
        return copy(
            send_ref.at[to, part], rx[part].at[slot], xsend.at[part, d], xrecv.at[part, slot], {"tmpl": to}
        )

    def acopy(d, slot):
        to = {"tm": lax.rem(my + d, PARTS)}
        return copy(pa_ref.at[my], pa_ref.at[slot], asend.at[d], arecv.at[slot], to)

    def hcopy():
        return copy(hs_ref, hr_ref, hsend, hrecv, {"tm": lax.rem(my + PARTS - 1, PARTS)})

    def lcopy(d, slot):
        to = {"tm": lax.rem(my + d, PARTS)}
        return copy(ls_ref, la_ref.at[slot], lsend.at[d], lrecv.at[slot], to)

    def part_back(d):
        return lax.rem(my + PARTS - d, PARTS)

    bar = pltpu.get_barrier_semaphore()
    loop(HOMES, lambda d: pl.semaphore_signal(bar, inc=1, device_id={"tmpl": home(d)}, device_id_type=MESH))
    loop(
        PARTS,
        lambda d: pl.semaphore_signal(
            bar, inc=1, device_id={"tm": lax.rem(my + d, PARTS)}, device_id_type=MESH
        ),
    )
    pl.semaphore_wait(bar, HOMES + PARTS - 2)

    loop(PARTS, lambda d: tcopy(d, my).start())
    loop(HOMES, lambda d: pcopy(d, me).start())
    loop(HOMES, lambda d: xcopy(d, 0, me).start())
    loop(HOMES, lambda d: xcopy(d, 1, me).start())

    tg_ref[my] = tl_ref[...]
    pa_ref[my, me] = pw_ref[me]
    for part in range(2):
        for i in range(2):
            for c in range(CHANS):
                rx[part][me, i, c] = send_ref[me, part, i, c]
    for s in range(8):
        tsb_ref[s] = jnp.broadcast_to(ts_ref[:, s : s + 1], (TPL, 128))

    def ohstep(j, _):
        m = gs_ref[me, j]
        for s in range(8):
            oh_ref[j, s] = jnp.where(tsb_ref[s] == m, 1.0, 0.0).astype(BF)
        return 0

    lax.fori_loop(0, MEMBERS, ohstep, 0)

    loop(PARTS, lambda d: tcopy(d, part_back(d)).wait_recv())

    def tstep(n, _):
        for b in range(PARTS):
            tf_ref[n, 4 * b : 4 * b + 4, :] = tg_ref[b, n].astype(F32)
        t_ref[n] = tf_ref[n].astype(BF)
        return 0

    lax.fori_loop(0, 24, tstep, 0)

    loop(HOMES, lambda d: pcopy(d, back(d)).wait_recv())
    loop(PARTS, lambda d: acopy(d, my).start())

    bits = lane_bits(16)
    w0_ref[NV - 1] = jnp.zeros_like(w0_ref[NV - 1])
    p8_ref[0] = jnp.zeros_like(p8_ref[0])

    def gstep(i, _):
        g, kh = i // 2, i % 2
        c, jh = g // 2, g % 2
        k0 = pl.multiple_of(kh * 16, 16)
        for t in range(4):
            tt = [t_ref[s * 3 + c, pl.ds(k0, 16), t * 128 : t * 128 + 128] for s in range(8)]
            tiles = []
            for jl in range(16):
                pr = [oh_ref[jh * 16 + jl, s, pl.ds(k0, 16), :] * tt[s] for s in range(8)]
                while len(pr) > 1:
                    pr = [pr[2 * n] + pr[2 * n + 1] for n in range(len(pr) // 2)]
                tiles.append(pr[0])
            y = swap_blocks(tiles, bits)
            for b in range(16 if t < 3 else 2):
                w0_ref[16 * t + b, g, pl.ds(k0, 16), :] = y[b]
                p8_ref[16 * t + b + 1, g, pl.ds(k0, 16), :] = lroll(y[b], -8)
        return 0

    lax.fori_loop(0, 12, gstep, 0)

    loop(HOMES, lambda d: xcopy(d, 0, back(d)).wait_recv())

    def slot_of(j):
        h = gs_ref[me, j] // STA
        same = (j > 0) & (gs_ref[me, jnp.maximum(j - 1, 0)] // STA == h)
        return h, jnp.where(same, 1, 0)

    def hstep(j, _):
        h, i = slot_of(j)
        for c in range(CHANS):
            hs_ref[j, c] = r0_ref[h, i, c]
        return 0

    lax.fori_loop(0, MEMBERS, hstep, 0)
    hcopy().start()

    low = (lax.broadcasted_iota(jnp.int32, (32, 128), 1) & 7).astype(F32).astype(BF)

    def vstep(v, _):
        for r in range(8):
            keep = low < BF(8 - r) if r else None
            for u in range(VU):
                for g in range(6):
                    z = w0_ref[v * VU + u, g]
                    if r:
                        z = lroll(jnp.where(keep, z, p8_ref[v * VU + u, g]), r)
                    w_ref[v * VU + u, r * 32 : r * 32 + 32, g * 128 : g * 128 + 128] = z
        return 0

    lax.fori_loop(0, NV // VU, vstep, 0)

    loop(PARTS, lambda d: acopy(d, part_back(d)).wait_recv())
    for h in range(HOMES):
        s = pa_ref[0, h]
        for b in range(1, PARTS):
            s = s + pa_ref[b, h]
        p2_ref[h : h + 1, :] = s
    inv = 1.0 / jnp.sqrt(p2_ref[...] / SAMPLES + 1e-06)
    for n in range(6):
        inv_ref[n] = jnp.broadcast_to(inv[:, n : n + 1], (HOMES, 128))

    loop(HOMES, lambda d: xcopy(d, 1, back(d)).wait_recv())
    hcopy().wait_recv()
    ahead = jnp.where(my < PARTS - 1, 1.0, 0.0)

    bits2 = lane_bits(32)

    def estep(g, _):
        c, jh = g // 2, g % 2
        tiles = []
        for jl in range(16):
            j = jh * 16 + jl
            h, i = slot_of(j)
            x = jnp.concatenate(
                [
                    r0_ref[h, i, c].astype(F32),
                    r1_ref[h, i, c].astype(F32),
                    hr_ref[j, c].astype(F32) * ahead,
                ],
                axis=0,
            )
            x = x * inv_ref[c * 2 + i, pl.ds(h, 1), :]
            tiles.append(jnp.concatenate([x, jnp.zeros((8, 128), F32)], axis=0).astype(BF))
        y = swap_blocks(tiles, bits2)
        for p in range(16):
            yf_ref[p, g] = y[p][0:24].astype(F32)
        return 0

    lax.fori_loop(0, 6, estep, 0)

    def pstep(p, _):
        for g in range(6):
            for m in range(4):
                at = pl.ds(pl.multiple_of((m * 16 + p) * 16, 16), 16)
                e_ref[at, g * 128 : g * 128 + 128] = yf_ref[p, g, m : m + 16, :].astype(BF)
        return 0

    lax.fori_loop(0, 16, pstep, 0)
    for p in range(3):
        for g in range(6):
            at = (64 + p) * 16
            e_ref[at : at + 16, g * 128 : g * 128 + 128] = yf_ref[p, g, 4:20, :].astype(BF)

    o_ref[...] = jnp.zeros_like(o_ref)

    def dstep(n, _):
        rows = [e_ref[pl.ds(pl.multiple_of((n * VD + i) * 16, 16), 256), :] for i in range(VD)]
        cols = [w_ref[n * VD + i] for i in range(VD)]
        o_ref[...] += lax.dot_general(
            jnp.concatenate(rows, axis=1),
            jnp.concatenate(cols, axis=1),
            (((1,), (1,)), ((), ())),
            preferred_element_type=F32,
        )
        return 0

    lax.fori_loop(0, NV // VD, dstep, 0)

    a = o_ref[...]
    s = jnp.sum(a * a, axis=0, keepdims=True)
    s = jnp.broadcast_to(s[:, :128] + s[:, 128:], (8, 128))
    s = s + lroll(s, 64)
    s = s + lroll(s, 32)
    ls_ref[...] = s
    la_ref[my] = s
    loop(PARTS, lambda d: lcopy(d, my).start())
    loop(PARTS, lambda d: lcopy(d, part_back(d)).wait_recv())
    level = la_ref[0]
    for b in range(1, PARTS):
        level = level + la_ref[b]
    scale = 1.0 / jnp.sqrt(level[0:1, :] / SAMPLES + 1e-06)
    o_ref[:, :128] = a[:, :128] * scale
    o_ref[:, 128:] = a[:, 128:] * scale

    loop(PARTS, lambda d: tcopy(d, my).wait_send())
    loop(HOMES, lambda d: pcopy(d, me).wait_send())
    loop(HOMES, lambda d: xcopy(d, 0, me).wait_send())
    loop(HOMES, lambda d: xcopy(d, 1, me).wait_send())
    loop(PARTS, lambda d: acopy(d, my).wait_send())
    hcopy().wait_send()
    loop(PARTS, lambda d: lcopy(d, my).wait_send())


def detect(gs, ts, tl, send, pw):
    smem = pl.BlockSpec(memory_space=pltpu.SMEM)
    vmem = pl.BlockSpec(memory_space=pltpu.VMEM)
    dma = pltpu.SemaphoreType.DMA
    return pl.pallas_call(
        main_kernel,
        out_shape=jax.ShapeDtypeStruct((256, 256), F32),
        in_specs=[smem, vmem, vmem, vmem, vmem],
        out_specs=vmem,
        scratch_shapes=[
            pltpu.VMEM((NV, 256, 768), BF),
            pltpu.VMEM((NV, 6, 32, 128), BF),
            pltpu.VMEM((NV, 6, 32, 128), BF),
            pltpu.VMEM((NROW, 768), BF),
            pltpu.VMEM((16, 6, 24, 128), F32),
            pltpu.VMEM((MEMBERS, 8, TPL, 128), BF),
            pltpu.VMEM((8, TPL, 128), jnp.int32),
            pltpu.VMEM((PARTS, 24, 4, 512), BF),
            pltpu.VMEM((24, TPL, 512), F32),
            pltpu.VMEM((24, TPL, 512), BF),
            pltpu.VMEM((HOMES, 2, CHANS, 8, 128), BF),
            pltpu.VMEM((HOMES, 2, CHANS, 8, 128), BF),
            pltpu.VMEM((MEMBERS, CHANS, 8, 128), BF),
            pltpu.VMEM((MEMBERS, CHANS, 8, 128), BF),
            pltpu.VMEM((PARTS, HOMES, 1, 128), F32),
            pltpu.VMEM((HOMES, 128), F32),
            pltpu.VMEM((6, HOMES, 128), F32),
            pltpu.VMEM((8, 128), F32),
            pltpu.VMEM((PARTS, 8, 128), F32),
            dma((PARTS,)), dma((PARTS,)),
            dma((HOMES,)), dma((HOMES,)),
            dma((2, HOMES)), dma((2, HOMES)),
            dma((PARTS,)), dma((PARTS,)),
            dma, dma,
            dma((PARTS,)), dma((PARTS,)),
        ],
        compiler_params=pltpu.CompilerParams(
            vmem_limit_bytes=56 << 20, collective_id=0, has_side_effects=True
        ),
    )(gs, ts, tl, send, pw)


def body(traces, group_stations, template_stations, templates):
    send, pw, tl = pick_rows(group_stations, traces.transpose(1, 0, 2), templates)
    o = detect(group_stations, template_stations, tl, send, pw)
    out = o.reshape(16, 16, 8, TPL).transpose(3, 1, 0, 2).reshape(TPL, traces.shape[2])
    return out.astype(BF)


def solution(mesh):
    placed = (P("tmpl", None, "tm"), P(), P("tmpl", None), P(("tmpl", "tm"), None))
    return jax.shard_map(
        body, mesh=mesh, in_specs=placed, out_specs=P("tmpl", "tm"), check_vma=False
    )
```

```python
import jax
import jax.numpy as jnp
from jax import lax
from jax.experimental import pallas as pl
from jax.experimental.pallas import tpu as pltpu
from jax.sharding import PartitionSpec as P

BF = jnp.bfloat16
F32 = jnp.float32
MESH = pl.DeviceIdType.MESH
HOMES, PARTS, STA, MEMBERS, TPL, CHANS = 32, 8, 64, 32, 32, 3
SAMPLES = 16384
NV = 51
NROW = 67 * 16
VU = 3
VD = 17


def lroll(x, s):
    s %= 128
    return x if s == 0 else pltpu.roll(x, s, 1)


def lane_bits(rows):
    lane = lax.broadcasted_iota(jnp.int32, (rows, 128), 1)
    return [((lane >> (3 + s)) & 1).astype(F32).astype(BF) > BF(0.5) for s in range(4)]


def swap_blocks(x, bits):
    x = list(x)
    for s in range(4):
        d = 1 << s
        y = list(x)
        for i in range(16):
            if i & d:
                continue
            a, b = x[i], x[i + d]
            y[i] = jnp.where(bits[s], lroll(b, 8 * d), a)
            y[i + d] = jnp.where(bits[s], b, lroll(a, -8 * d))
        x = y
    return x


def main_kernel(
    gs_ref, gv_ref, ts_ref, tr_hbm, tp_hbm, o_ref,
    w_ref, w0_ref, p8_ref, e_ref, yf_ref, oh_ref, tsb_ref, tg_ref, tf_ref, tb_ref, t_ref,
    tr_ref, rows_ref, pscr_ref, send_ref, pw_ref, acc_ref,
    rx_ref, hs_ref, hr_ref, pa_ref, p2_ref, inv_ref, ls_ref, la_ref,
    inload, tsend, trecv, psend, precv, xsend, xrecv, asend, arecv, hsend, hrecv, lsend, lrecv,
):
    me = lax.axis_index("tmpl")
    my = lax.axis_index("tm")
    twin = my + 1 - 2 * lax.rem(my, 2)

    def home(d):
        z = lax.rem(me // 4 + d // 4, 8)
        return z * 4 + lax.rem(me % 4 + d % 4, 4)

    def back(d):
        z = lax.rem(me // 4 + 8 - d // 4, 8)
        return z * 4 + lax.rem(me % 4 + 4 - d % 4, 4)

    def part(d):
        return lax.rem(my + d, PARTS)

    def part_back(d):
        return lax.rem(my + PARTS - d, PARTS)

    def loop(n, f):
        def step(d, _):
            f(d)
            return 0

        lax.fori_loop(1, n, step, 0)

    def copy(src, dst, send, recv, to):
        return pltpu.make_async_remote_copy(
            src_ref=src, dst_ref=dst, send_sem=send, recv_sem=recv, device_id=to, device_id_type=MESH
        )

    def tcopy(d, slot):
        return copy(tg_ref.at[my], tg_ref.at[slot], tsend.at[d], trecv.at[slot], {"tm": part(2 * d)})

    def fcopy(d, slot):
        return copy(tg_ref.at[slot], tg_ref.at[slot], tsend.at[4 + d], trecv.at[slot], {"tm": twin})

    def pcopy(d, slot):
        to = home(d)
        return copy(pw_ref.at[to], pa_ref.at[my, slot], psend.at[d], precv.at[slot], {"tmpl": to})

    def xcopy(d, slot):
        to = home(d)
        return copy(send_ref.at[to], rx_ref.at[slot], xsend.at[d], xrecv.at[slot], {"tmpl": to})

    def acopy(d, slot):
        return copy(pa_ref.at[my], pa_ref.at[slot], asend.at[d], arecv.at[slot], {"tm": part(d)})

    def hcopy():
        return copy(hs_ref, hr_ref, hsend, hrecv, {"tm": part(PARTS - 1)})

    def lcopy(d, slot):
        return copy(ls_ref, la_ref.at[slot], lsend.at[d], lrecv.at[slot], {"tm": part(d)})

    tin = pltpu.make_async_copy(tp_hbm, tg_ref.at[my], inload.at[0])
    xin = pltpu.make_async_copy(tr_hbm, tr_ref, inload.at[1])
    xin.start()
    tin.start()

    bar = pltpu.get_barrier_semaphore()
    loop(HOMES, lambda d: pl.semaphore_signal(bar, inc=1, device_id={"tmpl": home(d)}, device_id_type=MESH))
    loop(PARTS, lambda d: pl.semaphore_signal(bar, inc=1, device_id={"tm": part(d)}, device_id_type=MESH))

    local = (gv_ref[...] - me * STA).astype(F32)
    mine = (local >= 0) & (local < STA)
    low = jnp.min(jnp.where(mine, local, 1e6), axis=1, keepdims=True)
    high = jnp.max(jnp.where(mine, local, -1.0), axis=1, keepdims=True)
    high = jnp.where(high > low, high, -2.0)
    row = lax.broadcasted_iota(jnp.int32, (HOMES, STA), 1).astype(F32)
    pick = jnp.concatenate([(row == low).astype(F32), (row == high).astype(F32)], axis=0).astype(BF)
    lane = lax.broadcasted_iota(jnp.int32, (HOMES, 128), 1)
    power = jnp.zeros((HOMES, 128), F32)
    xin.wait()
    for c in range(CHANS):
        sq = jnp.zeros((64, 128), F32)
        for ch in range(4):
            res = jnp.dot(
                pick, tr_ref[c, :, ch * 512 : ch * 512 + 512], preferred_element_type=F32
            )
            for n in range(4):
                v = res[:, n * 128 : n * 128 + 128]
                sq = sq + v * v
                rows_ref[c, pl.ds(ch * 4 + n, 64, stride=16), :] = v
        tot = jnp.sum(sq, axis=1, keepdims=True)
        for i in range(2):
            power = jnp.where(lane == c * 2 + i, tot[i * 32 : i * 32 + 32], power)
    pscr_ref[...] = power

    def pack(g, _):
        for i in range(2):
            for c in range(CHANS):
                at = pl.ds(pl.multiple_of((i * 32 + g) * 16, 16), 16)
                send_ref[g, i, c] = rows_ref[c, at, :].astype(BF)
        pw_ref[g] = pscr_ref[pl.ds(g, 1), :]
        return 0

    lax.fori_loop(0, HOMES, pack, 0, unroll=4)
    tin.wait()
    pl.semaphore_wait(bar, HOMES + PARTS - 2)

    for d in range(1, 4):
        tcopy(d, my).start()
    fcopy(0, my).start()
    loop(HOMES, lambda d: pcopy(d, me).start())
    loop(HOMES, lambda d: xcopy(d, me).start())

    pa_ref[my, me] = pw_ref[me]
    for i in range(2):
        for c in range(CHANS):
            rx_ref[me, i, c] = send_ref[me, i, c]
    diag = lax.broadcasted_iota(jnp.int32, (TPL, TPL), 0) == lax.broadcasted_iota(
        jnp.int32, (TPL, TPL), 1
    )
    for s in range(8):
        ids = jnp.broadcast_to(ts_ref[s : s + 1, :], (TPL, TPL)).astype(F32)
        ids = jnp.sum(jnp.where(diag, ids, 0.0), axis=1, keepdims=True)
        tsb_ref[s] = jnp.broadcast_to(ids, (TPL, 128))

    def ohstep(j, _):
        m = gs_ref[me, j].astype(F32)
        for s in range(8):
            oh_ref[j, s] = jnp.where(tsb_ref[s] == m, 1.0, 0.0).astype(BF)
        return 0

    lax.fori_loop(0, MEMBERS, ohstep, 0)

    for d in range(1, 4):
        tcopy(d, part_back(2 * d)).wait_recv()
        fcopy(d, part_back(2 * d)).start()
    for d in range(4):
        fcopy(d, lax.rem(twin + PARTS - 2 * d, PARTS)).wait_recv()

    def tstep(n, _):
        at = pl.ds(pl.multiple_of(n * 384, 128), 384)
        for b in range(PARTS):
            tf_ref[4 * b : 4 * b + 4, at] = tg_ref[b, :, at].astype(F32)
        tb_ref[:, at] = tf_ref[:, at].astype(BF)
        return 0

    lax.fori_loop(0, 25, tstep, 0)
    for n in range(24):
        t = tb_ref[:, n * 400 : n * 400 + 400]
        t_ref[n] = jnp.concatenate([t, jnp.zeros((TPL, 112), BF)], axis=1)

    loop(HOMES, lambda d: pcopy(d, back(d)).wait_recv())
    loop(PARTS, lambda d: acopy(d, my).start())

    bits = lane_bits(16)
    w0_ref[NV - 1] = jnp.zeros_like(w0_ref[NV - 1])
    p8_ref[0] = jnp.zeros_like(p8_ref[0])

    def gstep(i, _):
        g, kh = i // 2, i % 2
        c, jh = g // 2, g % 2
        k0 = pl.multiple_of(kh * 16, 16)
        for t in range(4):
            tt = [t_ref[s * 3 + c, pl.ds(k0, 16), t * 128 : t * 128 + 128] for s in range(8)]
            tiles = []
            for jl in range(16):
                pr = [oh_ref[jh * 16 + jl, s, pl.ds(k0, 16), :] * tt[s] for s in range(8)]
                while len(pr) > 1:
                    pr = [pr[2 * n] + pr[2 * n + 1] for n in range(len(pr) // 2)]
                tiles.append(pr[0])
            y = swap_blocks(tiles, bits)
            for b in range(16 if t < 3 else 2):
                w0_ref[16 * t + b, g, pl.ds(k0, 16), :] = y[b]
                p8_ref[16 * t + b + 1, g, pl.ds(k0, 16), :] = lroll(y[b], -8)
        return 0

    lax.fori_loop(0, 12, gstep, 0)

    loop(HOMES, lambda d: xcopy(d, back(d)).wait_recv())

    def slot_of(j):
        h = gs_ref[me, j] // STA
        same = (j > 0) & (gs_ref[me, jnp.maximum(j - 1, 0)] // STA == h)
        return h, jnp.where(same, 1, 0)

    def hstep(j, _):
        h, i = slot_of(j)
        for c in range(CHANS):
            hs_ref[j, c] = rx_ref[h, i, c, 0:8, :]
        return 0

    lax.fori_loop(0, MEMBERS, hstep, 0)
    hcopy().start()

    eighth = (lax.broadcasted_iota(jnp.int32, (32, 128), 1) & 7).astype(F32).astype(BF)

    def vstep(v, _):
        for r in range(8):
            keep = eighth < BF(8 - r) if r else None
            for u in range(VU):
                for g in range(6):
                    z = w0_ref[v * VU + u, g]
                    if r:
                        z = lroll(jnp.where(keep, z, p8_ref[v * VU + u, g]), r)
                    w_ref[v * VU + u, r * 32 : r * 32 + 32, g * 128 : g * 128 + 128] = z
        return 0

    lax.fori_loop(0, NV // VU, vstep, 0)

    loop(PARTS, lambda d: acopy(d, part_back(d)).wait_recv())
    for h in range(HOMES):
        s = pa_ref[0, h]
        for b in range(1, PARTS):
            s = s + pa_ref[b, h]
        p2_ref[h : h + 1, :] = s
    inv = 1.0 / jnp.sqrt(p2_ref[...] / SAMPLES + 1e-06)
    for n in range(6):
        inv_ref[n] = jnp.broadcast_to(inv[:, n : n + 1], (HOMES, 128))

    hcopy().wait_recv()
    ahead = jnp.where(my < PARTS - 1, 1.0, 0.0)

    bits2 = lane_bits(32)

    def estep(g, _):
        c, jh = g // 2, g % 2
        tiles = []
        for jl in range(16):
            j = jh * 16 + jl
            h, i = slot_of(j)
            x = jnp.concatenate(
                [
                    rx_ref[h, i, c].astype(F32),
                    hr_ref[j, c].astype(F32) * ahead,
                ],
                axis=0,
            )
            x = x * inv_ref[c * 2 + i, pl.ds(h, 1), :]
            tiles.append(jnp.concatenate([x, jnp.zeros((8, 128), F32)], axis=0).astype(BF))
        y = swap_blocks(tiles, bits2)
        for p in range(16):
            yf_ref[p, g] = y[p][0:24].astype(F32)
        return 0

    lax.fori_loop(0, 6, estep, 0)

    def pstep(p, _):
        for g in range(6):
            for m in range(4):
                at = pl.ds(pl.multiple_of((m * 16 + p) * 16, 16), 16)
                e_ref[at, g * 128 : g * 128 + 128] = yf_ref[p, g, m : m + 16, :].astype(BF)
        return 0

    lax.fori_loop(0, 16, pstep, 0)
    for p in range(3):
        for g in range(6):
            at = (64 + p) * 16
            e_ref[at : at + 16, g * 128 : g * 128 + 128] = yf_ref[p, g, 4:20, :].astype(BF)

    acc_ref[...] = jnp.zeros_like(acc_ref)

    def dstep(n, _):
        rows = [e_ref[pl.ds(pl.multiple_of((n * VD + i) * 16, 16), 256), :] for i in range(VD)]
        cols = [w_ref[n * VD + i] for i in range(VD)]
        acc_ref[...] += lax.dot_general(
            jnp.concatenate(rows, axis=1),
            jnp.concatenate(cols, axis=1),
            (((1,), (1,)), ((), ())),
            preferred_element_type=F32,
        )
        return 0

    lax.fori_loop(0, NV // VD, dstep, 0)

    a = acc_ref[...]
    s = jnp.sum(a * a, axis=0, keepdims=True)
    s = jnp.broadcast_to(s[:, :128] + s[:, 128:], (8, 128))
    s = s + lroll(s, 64)
    s = s + lroll(s, 32)
    ls_ref[...] = s
    la_ref[my] = s
    loop(PARTS, lambda d: lcopy(d, my).start())

    for d in range(1, 4):
        tcopy(d, my).wait_send()
    for d in range(4):
        fcopy(d, part_back(2 * d)).wait_send()
    loop(HOMES, lambda d: pcopy(d, me).wait_send())
    loop(HOMES, lambda d: xcopy(d, me).wait_send())
    loop(PARTS, lambda d: acopy(d, my).wait_send())
    hcopy().wait_send()

    loop(PARTS, lambda d: lcopy(d, part_back(d)).wait_recv())
    level = la_ref[0]
    for b in range(1, PARTS):
        level = level + la_ref[b]
    scale = 1.0 / jnp.sqrt(level[0:1, :] / SAMPLES + 1e-06)
    a = acc_ref[...]
    o_ref[:, :128] = (a[:, :128] * scale).astype(BF)
    o_ref[:, 128:] = (a[:, 128:] * scale).astype(BF)
    loop(PARTS, lambda d: lcopy(d, my).wait_send())


def detect(gs, ts, traces, templates):
    smem = pl.BlockSpec(memory_space=pltpu.SMEM)
    vmem = pl.BlockSpec(memory_space=pltpu.VMEM)
    hbm = pl.BlockSpec(memory_space=pltpu.HBM)
    dma = pltpu.SemaphoreType.DMA
    return pl.pallas_call(
        main_kernel,
        out_shape=jax.ShapeDtypeStruct((256, 256), BF),
        in_specs=[smem, vmem, vmem, hbm, hbm],
        out_specs=vmem,
        scratch_shapes=[
            pltpu.VMEM((NV, 256, 768), BF),
            pltpu.VMEM((NV, 6, 32, 128), BF),
            pltpu.VMEM((NV, 6, 32, 128), BF),
            pltpu.VMEM((NROW, 768), BF),
            pltpu.VMEM((16, 6, 24, 128), F32),
            pltpu.VMEM((MEMBERS, 8, TPL, 128), BF),
            pltpu.VMEM((8, TPL, 128), F32),
            pltpu.VMEM((PARTS, 4, 9600), BF),
            pltpu.VMEM((TPL, 9600), F32),
            pltpu.VMEM((TPL, 9600), BF),
            pltpu.VMEM((24, TPL, 512), BF),
            pltpu.VMEM((CHANS, STA, 2048), BF),
            pltpu.VMEM((CHANS, 1024, 128), F32),
            pltpu.VMEM((HOMES, 128), F32),
            pltpu.VMEM((HOMES, 2, CHANS, 16, 128), BF),
            pltpu.VMEM((HOMES, 1, 128), F32),
            pltpu.VMEM((256, 256), F32),
            pltpu.VMEM((HOMES, 2, CHANS, 16, 128), BF),
            pltpu.VMEM((MEMBERS, CHANS, 8, 128), BF),
            pltpu.VMEM((MEMBERS, CHANS, 8, 128), BF),
            pltpu.VMEM((PARTS, HOMES, 1, 128), F32),
            pltpu.VMEM((HOMES, 128), F32),
            pltpu.VMEM((6, HOMES, 128), F32),
            pltpu.VMEM((8, 128), F32),
            pltpu.VMEM((PARTS, 8, 128), F32),
            dma((2,)),
            dma((PARTS,)), dma((PARTS,)),
            dma((HOMES,)), dma((HOMES,)),
            dma((HOMES,)), dma((HOMES,)),
            dma((PARTS,)), dma((PARTS,)),
            dma, dma,
            dma((PARTS,)), dma((PARTS,)),
        ],
        compiler_params=pltpu.CompilerParams(
            vmem_limit_bytes=56 << 20, collective_id=0, has_side_effects=True
        ),
    )(gs, gs, ts, traces, templates)


def body(traces, group_stations, template_stations, templates):
    o = detect(group_stations, template_stations.T, traces.transpose(1, 0, 2), templates)
    return o.reshape(16, 16, 8, TPL).transpose(3, 1, 0, 2).reshape(TPL, traces.shape[2])


def solution(mesh):
    placed = (P("tmpl", None, "tm"), P(), P("tmpl", None), P(("tmpl", "tm"), None))
    return jax.shard_map(
        body, mesh=mesh, in_specs=placed, out_specs=P("tmpl", "tm"), check_vma=False
    )
```

```python
import jax
import jax.numpy as jnp
from jax import lax
from jax.experimental import pallas as pl
from jax.experimental.pallas import tpu as pltpu
from jax.sharding import PartitionSpec as P

BF = jnp.bfloat16
F32 = jnp.float32
MESH = pl.DeviceIdType.MESH
HOMES, PARTS, STA, MEMBERS, TPL, CHANS = 32, 8, 64, 32, 32, 3
SAMPLES = 16384
NV = 51
NROW = 67 * 16
VU = 3
VD = 17


def lroll(x, s):
    s %= 128
    return x if s == 0 else pltpu.roll(x, s, 1)


def lane_bits(rows):
    lane = lax.broadcasted_iota(jnp.int32, (rows, 128), 1)
    return [((lane >> (3 + s)) & 1).astype(F32).astype(BF) > BF(0.5) for s in range(4)]


def swap_blocks(x, bits):
    x = list(x)
    for s in range(4):
        d = 1 << s
        y = list(x)
        for i in range(16):
            if i & d:
                continue
            a, b = x[i], x[i + d]
            y[i] = jnp.where(bits[s], lroll(b, 8 * d), a)
            y[i + d] = jnp.where(bits[s], b, lroll(a, -8 * d))
        x = y
    return x


def main_kernel(
    gs_ref, gv_ref, ts_ref, tr_hbm, tp_hbm, o_ref,
    w_ref, w0_ref, p8_ref, e_ref, yf_ref, oh_ref, tsb_ref, tg_ref, tf_ref, tb_ref, t_ref,
    tr_ref, rows_ref, pscr_ref, send_ref, pw_ref, acc_ref,
    r0_ref, r1_ref, hs_ref, hr_ref, pa_ref, p2_ref, inv_ref, ls_ref, la_ref,
    inload, tsend, trecv, psend, precv, xsend, xrecv, asend, arecv, hsend, hrecv, lsend, lrecv,
):
    me = lax.axis_index("tmpl")
    my = lax.axis_index("tm")
    rx = (r0_ref, r1_ref)
    twin = my + 1 - 2 * lax.rem(my, 2)

    def hop(d):
        i = lax.rem(8 - d % 8, 8)
        z = (i + 1) // 2 * (2 * (i % 2) - 1)
        return z, d // 8

    def home(d):
        z, x = hop(d)
        return lax.rem(me // 4 + 8 + z, 8) * 4 + lax.rem(me % 4 + x, 4)

    def back(d):
        z, x = hop(d)
        return lax.rem(me // 4 + 8 - z, 8) * 4 + lax.rem(me % 4 + 4 - x, 4)

    def part(d):
        return lax.rem(my + d, PARTS)

    def part_back(d):
        return lax.rem(my + PARTS - d, PARTS)

    def loop(n, f):
        def step(d, _):
            f(d)
            return 0

        lax.fori_loop(1, n, step, 0)

    def copy(src, dst, send, recv, to):
        return pltpu.make_async_remote_copy(
            src_ref=src, dst_ref=dst, send_sem=send, recv_sem=recv, device_id=to, device_id_type=MESH
        )

    def tcopy(d, slot):
        return copy(tg_ref.at[my], tg_ref.at[slot], tsend.at[d], trecv.at[slot], {"tm": part(2 * d)})

    def fcopy(d, slot):
        return copy(tg_ref.at[slot], tg_ref.at[slot], tsend.at[4 + d], trecv.at[slot], {"tm": twin})

    def pcopy(d, slot):
        to = home(d)
        return copy(pw_ref.at[to], pa_ref.at[my, slot], psend.at[d], precv.at[slot], {"tmpl": to})

    def xcopy(d, half, slot):
        to = home(d)
        return copy(
            send_ref.at[to, half], rx[half].at[slot], xsend.at[half, d], xrecv.at[half, slot], {"tmpl": to}
        )

    def acopy(d, slot):
        return copy(pa_ref.at[my], pa_ref.at[slot], asend.at[d], arecv.at[slot], {"tm": part(d)})

    def hcopy():
        return copy(hs_ref, hr_ref, hsend, hrecv, {"tm": part(PARTS - 1)})

    def lcopy(d, slot):
        return copy(ls_ref, la_ref.at[slot], lsend.at[d], lrecv.at[slot], {"tm": part(d)})

    tin = pltpu.make_async_copy(tp_hbm, tg_ref.at[my], inload.at[0])
    xin = pltpu.make_async_copy(tr_hbm, tr_ref, inload.at[1])
    xin.start()
    tin.start()

    bar = pltpu.get_barrier_semaphore()
    loop(HOMES, lambda d: pl.semaphore_signal(bar, inc=1, device_id={"tmpl": home(d)}, device_id_type=MESH))
    loop(PARTS, lambda d: pl.semaphore_signal(bar, inc=1, device_id={"tm": part(d)}, device_id_type=MESH))

    local = (gv_ref[...] - me * STA).astype(F32)
    mine = (local >= 0) & (local < STA)
    low = jnp.min(jnp.where(mine, local, 1e6), axis=1, keepdims=True)
    high = jnp.max(jnp.where(mine, local, -1.0), axis=1, keepdims=True)
    high = jnp.where(high > low, high, -2.0)
    row = lax.broadcasted_iota(jnp.int32, (HOMES, STA), 1).astype(F32)
    pick = jnp.concatenate([(row == low).astype(F32), (row == high).astype(F32)], axis=0).astype(BF)
    lane = lax.broadcasted_iota(jnp.int32, (HOMES, 128), 1)
    power = jnp.zeros((HOMES, 128), F32)
    xin.wait()
    for c in range(CHANS):
        sq = jnp.zeros((64, 128), F32)
        for ch in range(4):
            res = jnp.dot(
                pick, tr_ref[c, :, ch * 512 : ch * 512 + 512], preferred_element_type=F32
            )
            for n in range(4):
                v = res[:, n * 128 : n * 128 + 128]
                sq = sq + v * v
                rows_ref[c, pl.ds(ch * 4 + n, 64, stride=16), :] = v
        tot = jnp.sum(sq, axis=1, keepdims=True)
        for i in range(2):
            power = jnp.where(lane == c * 2 + i, tot[i * 32 : i * 32 + 32], power)
    pscr_ref[...] = power

    def pack(g, _):
        for i in range(2):
            for c in range(CHANS):
                at = pl.ds(pl.multiple_of((i * 32 + g) * 16, 16), 16)
                v = rows_ref[c, at, :].astype(BF)
                send_ref[g, 0, i, c] = v[:8]
                send_ref[g, 1, i, c] = v[8:]
        pw_ref[g] = pscr_ref[pl.ds(g, 1), :]
        return 0

    lax.fori_loop(0, HOMES, pack, 0, unroll=4)
    tin.wait()
    pl.semaphore_wait(bar, HOMES + PARTS - 2)

    for d in range(1, 4):
        tcopy(d, my).start()
    fcopy(0, my).start()
    loop(HOMES, lambda d: xcopy(d, 0, me).start())
    loop(HOMES, lambda d: pcopy(d, me).start())
    loop(HOMES, lambda d: xcopy(d, 1, me).start())

    pa_ref[my, me] = pw_ref[me]
    for half in range(2):
        for i in range(2):
            for c in range(CHANS):
                rx[half][me, i, c] = send_ref[me, half, i, c]
    diag = lax.broadcasted_iota(jnp.int32, (TPL, TPL), 0) == lax.broadcasted_iota(
        jnp.int32, (TPL, TPL), 1
    )
    for s in range(8):
        ids = jnp.broadcast_to(ts_ref[s : s + 1, :], (TPL, TPL)).astype(F32)
        ids = jnp.sum(jnp.where(diag, ids, 0.0), axis=1, keepdims=True)
        tsb_ref[s] = jnp.broadcast_to(ids, (TPL, 128))

    def ohstep(j, _):
        m = gs_ref[me, j].astype(F32)
        for s in range(8):
            oh_ref[j, s] = jnp.where(tsb_ref[s] == m, 1.0, 0.0).astype(BF)
        return 0

    lax.fori_loop(0, MEMBERS, ohstep, 0)

    for d in range(1, 4):
        tcopy(d, part_back(2 * d)).wait_recv()
        fcopy(d, part_back(2 * d)).start()
    for d in range(4):
        fcopy(d, lax.rem(twin + PARTS - 2 * d, PARTS)).wait_recv()

    def tstep(n, _):
        at = pl.ds(pl.multiple_of(n * 384, 128), 384)
        for b in range(PARTS):
            tf_ref[4 * b : 4 * b + 4, at] = tg_ref[b, :, at].astype(F32)
        tb_ref[:, at] = tf_ref[:, at].astype(BF)
        return 0

    lax.fori_loop(0, 25, tstep, 0)
    for n in range(24):
        t = tb_ref[:, n * 400 : n * 400 + 400]
        t_ref[n] = jnp.concatenate([t, jnp.zeros((TPL, 112), BF)], axis=1)

    bits = lane_bits(16)
    w0_ref[NV - 1] = jnp.zeros_like(w0_ref[NV - 1])
    p8_ref[0] = jnp.zeros_like(p8_ref[0])

    def gstep(i, _):
        g, kh = i // 2, i % 2
        c, jh = g // 2, g % 2
        k0 = pl.multiple_of(kh * 16, 16)
        for t in range(4):
            tt = [t_ref[s * 3 + c, pl.ds(k0, 16), t * 128 : t * 128 + 128] for s in range(8)]
            tiles = []
            for jl in range(16):
                pr = [oh_ref[jh * 16 + jl, s, pl.ds(k0, 16), :] * tt[s] for s in range(8)]
                while len(pr) > 1:
                    pr = [pr[2 * n] + pr[2 * n + 1] for n in range(len(pr) // 2)]
                tiles.append(pr[0])
            y = swap_blocks(tiles, bits)
            for b in range(16 if t < 3 else 2):
                w0_ref[16 * t + b, g, pl.ds(k0, 16), :] = y[b]
                p8_ref[16 * t + b + 1, g, pl.ds(k0, 16), :] = lroll(y[b], -8)
        return 0

    lax.fori_loop(0, 12, gstep, 0)

    loop(HOMES, lambda d: xcopy(d, 0, back(d)).wait_recv())

    def slot_of(j):
        h = gs_ref[me, j] // STA
        same = (j > 0) & (gs_ref[me, jnp.maximum(j - 1, 0)] // STA == h)
        return h, jnp.where(same, 1, 0)

    def hstep(j, _):
        h, i = slot_of(j)
        for c in range(CHANS):
            hs_ref[j, c] = r0_ref[h, i, c]
        return 0

    lax.fori_loop(0, MEMBERS, hstep, 0)
    hcopy().start()

    loop(HOMES, lambda d: pcopy(d, back(d)).wait_recv())
    loop(PARTS, lambda d: acopy(d, my).start())

    eighth = (lax.broadcasted_iota(jnp.int32, (32, 128), 1) & 7).astype(F32).astype(BF)

    def vstep(v, _):
        for r in range(8):
            keep = eighth < BF(8 - r) if r else None
            for u in range(VU):
                for g in range(6):
                    z = w0_ref[v * VU + u, g]
                    if r:
                        z = lroll(jnp.where(keep, z, p8_ref[v * VU + u, g]), r)
                    w_ref[v * VU + u, r * 32 : r * 32 + 32, g * 128 : g * 128 + 128] = z
        return 0

    lax.fori_loop(0, NV // VU, vstep, 0)

    loop(PARTS, lambda d: acopy(d, part_back(d)).wait_recv())
    for h in range(HOMES):
        s = pa_ref[0, h]
        for b in range(1, PARTS):
            s = s + pa_ref[b, h]
        p2_ref[h : h + 1, :] = s
    inv = 1.0 / jnp.sqrt(p2_ref[...] / SAMPLES + 1e-06)
    for n in range(6):
        inv_ref[n] = jnp.broadcast_to(inv[:, n : n + 1], (HOMES, 128))

    loop(HOMES, lambda d: xcopy(d, 1, back(d)).wait_recv())
    hcopy().wait_recv()
    ahead = jnp.where(my < PARTS - 1, 1.0, 0.0)

    bits2 = lane_bits(32)

    def estep(g, _):
        c, jh = g // 2, g % 2
        tiles = []
        for jl in range(16):
            j = jh * 16 + jl
            h, i = slot_of(j)
            x = jnp.concatenate(
                [
                    r0_ref[h, i, c].astype(F32),
                    r1_ref[h, i, c].astype(F32),
                    hr_ref[j, c].astype(F32) * ahead,
                ],
                axis=0,
            )
            x = x * inv_ref[c * 2 + i, pl.ds(h, 1), :]
            tiles.append(jnp.concatenate([x, jnp.zeros((8, 128), F32)], axis=0).astype(BF))
        y = swap_blocks(tiles, bits2)
        for p in range(16):
            yf_ref[p, g] = y[p][0:24].astype(F32)
        return 0

    lax.fori_loop(0, 6, estep, 0)

    def pstep(p, _):
        for g in range(6):
            for m in range(4):
                at = pl.ds(pl.multiple_of((m * 16 + p) * 16, 16), 16)
                e_ref[at, g * 128 : g * 128 + 128] = yf_ref[p, g, m : m + 16, :].astype(BF)
        return 0

    lax.fori_loop(0, 16, pstep, 0)
    for p in range(3):
        for g in range(6):
            at = (64 + p) * 16
            e_ref[at : at + 16, g * 128 : g * 128 + 128] = yf_ref[p, g, 4:20, :].astype(BF)

    acc_ref[...] = jnp.zeros_like(acc_ref)

    def dstep(n, _):
        rows = [e_ref[pl.ds(pl.multiple_of((n * VD + i) * 16, 16), 256), :] for i in range(VD)]
        cols = [w_ref[n * VD + i] for i in range(VD)]
        acc_ref[...] += lax.dot_general(
            jnp.concatenate(rows, axis=1),
            jnp.concatenate(cols, axis=1),
            (((1,), (1,)), ((), ())),
            preferred_element_type=F32,
        )
        return 0

    lax.fori_loop(0, NV // VD, dstep, 0)

    a = acc_ref[...]
    s = jnp.sum(a * a, axis=0, keepdims=True)
    s = jnp.broadcast_to(s[:, :128] + s[:, 128:], (8, 128))
    s = s + lroll(s, 64)
    s = s + lroll(s, 32)
    ls_ref[...] = s
    la_ref[my] = s
    loop(PARTS, lambda d: lcopy(d, my).start())

    for d in range(1, 4):
        tcopy(d, my).wait_send()
    for d in range(4):
        fcopy(d, part_back(2 * d)).wait_send()
    loop(HOMES, lambda d: pcopy(d, me).wait_send())
    for half in range(2):
        loop(HOMES, lambda d: xcopy(d, half, me).wait_send())
    loop(PARTS, lambda d: acopy(d, my).wait_send())
    hcopy().wait_send()

    loop(PARTS, lambda d: lcopy(d, part_back(d)).wait_recv())
    level = la_ref[0]
    for b in range(1, PARTS):
        level = level + la_ref[b]
    scale = 1.0 / jnp.sqrt(level[0:1, :] / SAMPLES + 1e-06)
    a = acc_ref[...]
    o_ref[:, :128] = (a[:, :128] * scale).astype(BF)
    o_ref[:, 128:] = (a[:, 128:] * scale).astype(BF)
    loop(PARTS, lambda d: lcopy(d, my).wait_send())


def detect(gs, ts, traces, templates):
    smem = pl.BlockSpec(memory_space=pltpu.SMEM)
    vmem = pl.BlockSpec(memory_space=pltpu.VMEM)
    hbm = pl.BlockSpec(memory_space=pltpu.HBM)
    dma = pltpu.SemaphoreType.DMA
    return pl.pallas_call(
        main_kernel,
        out_shape=jax.ShapeDtypeStruct((256, 256), BF),
        in_specs=[smem, vmem, vmem, hbm, hbm],
        out_specs=vmem,
        scratch_shapes=[
            pltpu.VMEM((NV, 256, 768), BF),
            pltpu.VMEM((NV, 6, 32, 128), BF),
            pltpu.VMEM((NV, 6, 32, 128), BF),
            pltpu.VMEM((NROW, 768), BF),
            pltpu.VMEM((16, 6, 24, 128), F32),
            pltpu.VMEM((MEMBERS, 8, TPL, 128), BF),
            pltpu.VMEM((8, TPL, 128), F32),
            pltpu.VMEM((PARTS, 4, 9600), BF),
            pltpu.VMEM((TPL, 9600), F32),
            pltpu.VMEM((TPL, 9600), BF),
            pltpu.VMEM((24, TPL, 512), BF),
            pltpu.VMEM((CHANS, STA, 2048), BF),
            pltpu.VMEM((CHANS, 1024, 128), F32),
            pltpu.VMEM((HOMES, 128), F32),
            pltpu.VMEM((HOMES, 2, 2, CHANS, 8, 128), BF),
            pltpu.VMEM((HOMES, 1, 128), F32),
            pltpu.VMEM((256, 256), F32),
            pltpu.VMEM((HOMES, 2, CHANS, 8, 128), BF),
            pltpu.VMEM((HOMES, 2, CHANS, 8, 128), BF),
            pltpu.VMEM((MEMBERS, CHANS, 8, 128), BF),
            pltpu.VMEM((MEMBERS, CHANS, 8, 128), BF),
            pltpu.VMEM((PARTS, HOMES, 1, 128), F32),
            pltpu.VMEM((HOMES, 128), F32),
            pltpu.VMEM((6, HOMES, 128), F32),
            pltpu.VMEM((8, 128), F32),
            pltpu.VMEM((PARTS, 8, 128), F32),
            dma((2,)),
            dma((PARTS,)), dma((PARTS,)),
            dma((HOMES,)), dma((HOMES,)),
            dma((2, HOMES)), dma((2, HOMES)),
            dma((PARTS,)), dma((PARTS,)),
            dma, dma,
            dma((PARTS,)), dma((PARTS,)),
        ],
        compiler_params=pltpu.CompilerParams(
            vmem_limit_bytes=56 << 20, collective_id=0, has_side_effects=True
        ),
    )(gs, gs, ts, traces, templates)


def body(traces, group_stations, template_stations, templates):
    o = detect(group_stations, template_stations.T, traces.transpose(1, 0, 2), templates)
    return o.reshape(16, 16, 8, TPL).transpose(3, 1, 0, 2).reshape(TPL, traces.shape[2])


def solution(mesh):
    placed = (P("tmpl", None, "tm"), P(), P("tmpl", None), P(("tmpl", "tm"), None))
    return jax.shard_map(
        body, mesh=mesh, in_specs=placed, out_specs=P("tmpl", "tm"), check_vma=False
    )
```

```python
import jax
import jax.numpy as jnp
from jax import lax
from jax.experimental import pallas as pl
from jax.experimental.pallas import tpu as pltpu
from jax.sharding import PartitionSpec as P

BF = jnp.bfloat16
F32 = jnp.float32
MESH = pl.DeviceIdType.MESH
HOMES, PARTS, STA, MEMBERS, TPL, CHANS = 32, 8, 64, 32, 32, 3
SAMPLES = 16384
NV = 51
NROW = 67 * 16
VU = 3
VD = 17


def lroll(x, s):
    s %= 128
    return x if s == 0 else pltpu.roll(x, s, 1)


def lane_bits(rows):
    lane = lax.broadcasted_iota(jnp.int32, (rows, 128), 1)
    return [((lane >> (3 + s)) & 1).astype(F32).astype(BF) > BF(0.5) for s in range(4)]


def swap_blocks(x, bits):
    x = list(x)
    for s in range(4):
        d = 1 << s
        y = list(x)
        for i in range(16):
            if i & d:
                continue
            a, b = x[i], x[i + d]
            if d == 8:
                turned = lroll(jnp.where(bits[s], a, b), 64)
                y[i] = jnp.where(bits[s], turned, a)
                y[i + d] = jnp.where(bits[s], b, turned)
            else:
                y[i] = jnp.where(bits[s], lroll(b, 8 * d), a)
                y[i + d] = jnp.where(bits[s], b, lroll(a, -8 * d))
        x = y
    return x


def main_kernel(
    gs_ref, gv_ref, ts_ref, tr_hbm, tp_hbm, o_ref,
    w_ref, w0_ref, p8_ref, e_ref, yf_ref, oh_ref, spread_ref, ta_ref, tb2_ref, tsb_ref, tg_ref, tf_ref, tb_ref, t_ref,
    tr_ref, rows_ref, pscr_ref, send_ref, pw_ref, acc_ref,
    r0_ref, r1_ref, hs_ref, hr_ref, pa_ref, p2_ref, inv_ref, ls_ref, la_ref,
    inload, tsend, trecv, psend, precv, xsend, xrecv, asend, arecv, hsend, hrecv, lsend, lrecv,
):
    me = lax.axis_index("tmpl")
    my = lax.axis_index("tm")
    rx = (r0_ref, r1_ref)
    twin = my + 1 - 2 * lax.rem(my, 2)

    def hop(d):
        i = lax.rem(8 - d % 8, 8)
        z = (i + 1) // 2 * (2 * (i % 2) - 1)
        return z, d // 8

    def home(d):
        z, x = hop(d)
        return lax.rem(me // 4 + 8 + z, 8) * 4 + lax.rem(me % 4 + x, 4)

    def back(d):
        z, x = hop(d)
        return lax.rem(me // 4 + 8 - z, 8) * 4 + lax.rem(me % 4 + 4 - x, 4)

    def part(d):
        return lax.rem(my + d, PARTS)

    def part_back(d):
        return lax.rem(my + PARTS - d, PARTS)

    def loop(n, f):
        def step(d, _):
            f(d)
            return 0

        lax.fori_loop(1, n, step, 0)

    def copy(src, dst, send, recv, to):
        return pltpu.make_async_remote_copy(
            src_ref=src, dst_ref=dst, send_sem=send, recv_sem=recv, device_id=to, device_id_type=MESH
        )

    def tcopy(d, slot):
        return copy(tg_ref.at[my], tg_ref.at[slot], tsend.at[d], trecv.at[slot], {"tm": part(2 * d)})

    def fcopy(d, slot):
        return copy(tg_ref.at[slot], tg_ref.at[slot], tsend.at[4 + d], trecv.at[slot], {"tm": twin})

    def pcopy(d, slot):
        to = home(d)
        return copy(pw_ref.at[to], pa_ref.at[my, slot], psend.at[d], precv.at[slot], {"tmpl": to})

    def xcopy(d, half, slot):
        to = home(d)
        return copy(
            send_ref.at[to, half], rx[half].at[slot], xsend.at[half, d], xrecv.at[half, slot], {"tmpl": to}
        )

    def acopy(d, slot):
        return copy(pa_ref.at[my], pa_ref.at[slot], asend.at[d], arecv.at[slot], {"tm": part(d)})

    def hcopy():
        return copy(hs_ref, hr_ref, hsend, hrecv, {"tm": part(PARTS - 1)})

    def lcopy(d, slot):
        return copy(ls_ref, la_ref.at[slot], lsend.at[d], lrecv.at[slot], {"tm": part(d)})

    tin = pltpu.make_async_copy(tp_hbm, tg_ref.at[my], inload.at[0])
    xin = pltpu.make_async_copy(tr_hbm, tr_ref, inload.at[1])
    xin.start()
    tin.start()

    bar = pltpu.get_barrier_semaphore()
    loop(HOMES, lambda d: pl.semaphore_signal(bar, inc=1, device_id={"tmpl": home(d)}, device_id_type=MESH))
    loop(PARTS, lambda d: pl.semaphore_signal(bar, inc=1, device_id={"tm": part(d)}, device_id_type=MESH))

    local = (gv_ref[...] - me * STA).astype(F32)
    mine = (local >= 0) & (local < STA)
    low = jnp.min(jnp.where(mine, local, 1e6), axis=1, keepdims=True)
    high = jnp.max(jnp.where(mine, local, -1.0), axis=1, keepdims=True)
    high = jnp.where(high > low, high, -2.0)
    row = lax.broadcasted_iota(jnp.int32, (HOMES, STA), 1).astype(F32)
    pick = jnp.concatenate([(row == low).astype(F32), (row == high).astype(F32)], axis=0).astype(BF)
    lane = lax.broadcasted_iota(jnp.int32, (HOMES, 128), 1)
    power = jnp.zeros((HOMES, 128), F32)
    xin.wait()
    for c in range(CHANS):
        sq = jnp.zeros((64, 128), F32)
        for ch in range(4):
            res = jnp.dot(
                pick, tr_ref[c, :, ch * 512 : ch * 512 + 512], preferred_element_type=F32
            )
            for n in range(4):
                v = res[:, n * 128 : n * 128 + 128]
                sq = sq + v * v
                rows_ref[c, pl.ds(ch * 4 + n, 64, stride=16), :] = v
        tot = jnp.sum(sq, axis=1, keepdims=True)
        for i in range(2):
            power = jnp.where(lane == c * 2 + i, tot[i * 32 : i * 32 + 32], power)
    pscr_ref[...] = power

    def pack(g, _):
        for i in range(2):
            for c in range(CHANS):
                at = pl.ds(pl.multiple_of((i * 32 + g) * 16, 16), 16)
                v = rows_ref[c, at, :].astype(BF)
                send_ref[g, 0, i, c] = v[:8]
                send_ref[g, 1, i, c] = v[8:]
        pw_ref[g] = pscr_ref[pl.ds(g, 1), :]
        return 0

    lax.fori_loop(0, HOMES, pack, 0, unroll=4)
    tin.wait()
    pl.semaphore_wait(bar, HOMES + PARTS - 2)

    for d in range(1, 4):
        tcopy(d, my).start()
    fcopy(0, my).start()
    loop(HOMES, lambda d: xcopy(d, 0, me).start())
    loop(HOMES, lambda d: pcopy(d, me).start())
    loop(HOMES, lambda d: xcopy(d, 1, me).start())

    pa_ref[my, me] = pw_ref[me]
    for half in range(2):
        for i in range(2):
            for c in range(CHANS):
                rx[half][me, i, c] = send_ref[me, half, i, c]
    diag = lax.broadcasted_iota(jnp.int32, (TPL, TPL), 0) == lax.broadcasted_iota(
        jnp.int32, (TPL, TPL), 1
    )
    for s in range(8):
        ids = jnp.broadcast_to(ts_ref[s : s + 1, :], (TPL, TPL)).astype(F32)
        ids = jnp.sum(jnp.where(diag, ids, 0.0), axis=1, keepdims=True)
        tsb_ref[s] = jnp.broadcast_to(ids, (TPL, 128))

    block = lax.broadcasted_iota(jnp.int32, (TPL, 128), 1) >> 3
    for jh in range(2):
        ids = jnp.zeros((TPL, 128), F32)
        for jl in range(16):
            ids = jnp.where(block == jl, gs_ref[me, jh * 16 + jl].astype(F32), ids)
        for s in range(8):
            oh_ref[jh, s] = jnp.where(tsb_ref[s] == ids, 1.0, 0.0).astype(BF)
    row = lax.broadcasted_iota(jnp.int32, (128, 128), 0)
    lane = lax.broadcasted_iota(jnp.int32, (128, 128), 1) & 7
    for b in range(16):
        spread_ref[:, b * 128 : b * 128 + 128] = jnp.where(row == lane + 8 * b, 1.0, 0.0).astype(BF)

    for d in range(1, 4):
        tcopy(d, part_back(2 * d)).wait_recv()
        fcopy(d, part_back(2 * d)).start()
    for d in range(4):
        fcopy(d, lax.rem(twin + PARTS - 2 * d, PARTS)).wait_recv()

    def tstep(n, _):
        at = pl.ds(pl.multiple_of(n * 384, 128), 384)
        for b in range(PARTS):
            tf_ref[4 * b : 4 * b + 4, at] = tg_ref[b, :, at].astype(F32)
        tb_ref[:, at] = tf_ref[:, at].astype(BF)
        return 0

    lax.fori_loop(0, 25, tstep, 0)
    for n in range(24):
        t = tb_ref[:, n * 400 : n * 400 + 400]
        t_ref[n] = jnp.concatenate([t, jnp.zeros((TPL, 112), BF)], axis=1)

    w0_ref[NV - 1] = jnp.zeros_like(w0_ref[NV - 1])
    p8_ref[0] = jnp.zeros_like(p8_ref[0])

    def spread(t, to, blocks):
        for c in range(CHANS):
            x = [t_ref[s * CHANS + c, :, t * 128 : t * 128 + 128] for s in range(8)]
            x = jnp.concatenate(x, axis=0)
            x = jnp.dot(x, spread_ref[:, : blocks * 128], preferred_element_type=F32)
            to[c * 256 : c * 256 + 256, : blocks * 128] = x.astype(BF)

    def select(t, of, blocks):
        for kh in range(2):
            for jh in range(2):
                oh = [oh_ref[jh, s, kh * 16 : kh * 16 + 16, :] for s in range(8)]
                for b in range(blocks):
                    for c in range(CHANS):
                        pr = []
                        for s in range(8):
                            at = c * 256 + s * TPL + kh * 16
                            pr.append(oh[s] * of[at : at + 16, b * 128 : b * 128 + 128])
                        while len(pr) > 1:
                            pr = [pr[2 * n] + pr[2 * n + 1] for n in range(len(pr) // 2)]
                        w0_ref[16 * t + b, c * 2 + jh, kh * 16 : kh * 16 + 16, :] = pr[0]
                        p8_ref[16 * t + b + 1, c * 2 + jh, kh * 16 : kh * 16 + 16, :] = lroll(pr[0], -8)

    both = (ta_ref, tb2_ref)
    counts = (16, 16, 16, 2)
    spread(0, ta_ref, 16)
    for t in range(4):
        if t < 3:
            spread(t + 1, both[(t + 1) % 2], counts[t + 1])
        select(t, both[t % 2], counts[t])

    loop(HOMES, lambda d: xcopy(d, 0, back(d)).wait_recv())

    def slot_of(j):
        h = gs_ref[me, j] // STA
        same = (j > 0) & (gs_ref[me, jnp.maximum(j - 1, 0)] // STA == h)
        return h, jnp.where(same, 1, 0)

    def hstep(j, _):
        h, i = slot_of(j)
        for c in range(CHANS):
            hs_ref[j, c] = r0_ref[h, i, c]
        return 0

    lax.fori_loop(0, MEMBERS, hstep, 0)
    hcopy().start()

    loop(HOMES, lambda d: pcopy(d, back(d)).wait_recv())
    loop(PARTS, lambda d: acopy(d, my).start())

    eighth = (lax.broadcasted_iota(jnp.int32, (32, 128), 1) & 7).astype(F32).astype(BF)

    def vstep(v, _):
        for r in range(8):
            keep = eighth < BF(8 - r) if r else None
            for u in range(VU):
                for g in range(6):
                    z = w0_ref[v * VU + u, g]
                    if r:
                        z = lroll(jnp.where(keep, z, p8_ref[v * VU + u, g]), r)
                    w_ref[v * VU + u, r * 32 : r * 32 + 32, g * 128 : g * 128 + 128] = z
        return 0

    lax.fori_loop(0, NV // VU, vstep, 0)

    loop(PARTS, lambda d: acopy(d, part_back(d)).wait_recv())
    for h in range(HOMES):
        s = pa_ref[0, h]
        for b in range(1, PARTS):
            s = s + pa_ref[b, h]
        p2_ref[h : h + 1, :] = s
    inv = 1.0 / jnp.sqrt(p2_ref[...] / SAMPLES + 1e-06)
    for n in range(6):
        inv_ref[n] = jnp.broadcast_to(inv[:, n : n + 1], (HOMES, 128))

    loop(HOMES, lambda d: xcopy(d, 1, back(d)).wait_recv())
    hcopy().wait_recv()
    ahead = jnp.where(my < PARTS - 1, 1.0, 0.0)

    bits2 = lane_bits(48)

    def estep(c, _):
        tiles = []
        for jl in range(16):
            near, over = [], []
            for jh in range(2):
                j = jh * 16 + jl
                h, i = slot_of(j)
                at = inv_ref[c * 2 + i, pl.ds(h, 1), :]
                near.append(r0_ref[h, i, c].astype(F32) * at)
                near.append(r1_ref[h, i, c].astype(F32) * at)
                over.append(hr_ref[j, c].astype(F32) * (at * ahead))
            tiles.append(jnp.concatenate(near + over, axis=0).astype(BF))
        y = swap_blocks(tiles, bits2)
        for p in range(16):
            v = y[p].astype(F32)
            for jh in range(2):
                yf_ref[p, c * 2 + jh, 0:16, :] = v[16 * jh : 16 * jh + 16]
                yf_ref[p, c * 2 + jh, 16:24, :] = v[32 + 8 * jh : 40 + 8 * jh]
        return 0

    lax.fori_loop(0, CHANS, estep, 0)

    def pstep(p, _):
        for g in range(6):
            for m in range(4):
                at = pl.ds(pl.multiple_of((m * 16 + p) * 16, 16), 16)
                e_ref[at, g * 128 : g * 128 + 128] = yf_ref[p, g, m : m + 16, :].astype(BF)
        return 0

    lax.fori_loop(0, 16, pstep, 0)
    for p in range(3):
        for g in range(6):
            at = (64 + p) * 16
            e_ref[at : at + 16, g * 128 : g * 128 + 128] = yf_ref[p, g, 4:20, :].astype(BF)

    acc_ref[...] = jnp.zeros_like(acc_ref)

    def dstep(n, _):
        rows = [e_ref[pl.ds(pl.multiple_of((n * VD + i) * 16, 16), 256), :] for i in range(VD)]
        cols = [w_ref[n * VD + i] for i in range(VD)]
        acc_ref[...] += lax.dot_general(
            jnp.concatenate(rows, axis=1),
            jnp.concatenate(cols, axis=1),
            (((1,), (1,)), ((), ())),
            preferred_element_type=F32,
        )
        return 0

    lax.fori_loop(0, NV // VD, dstep, 0)

    a = acc_ref[...]
    s = jnp.sum(a * a, axis=0, keepdims=True)
    s = jnp.broadcast_to(s[:, :128] + s[:, 128:], (8, 128))
    s = s + lroll(s, 64)
    s = s + lroll(s, 32)
    ls_ref[...] = s
    la_ref[my] = s
    loop(PARTS, lambda d: lcopy(d, my).start())

    for d in range(1, 4):
        tcopy(d, my).wait_send()
    for d in range(4):
        fcopy(d, part_back(2 * d)).wait_send()
    loop(HOMES, lambda d: pcopy(d, me).wait_send())
    for half in range(2):
        loop(HOMES, lambda d: xcopy(d, half, me).wait_send())
    loop(PARTS, lambda d: acopy(d, my).wait_send())
    hcopy().wait_send()

    loop(PARTS, lambda d: lcopy(d, part_back(d)).wait_recv())
    level = la_ref[0]
    for b in range(1, PARTS):
        level = level + la_ref[b]
    scale = 1.0 / jnp.sqrt(level[0:1, :] / SAMPLES + 1e-06)
    a = acc_ref[...]
    o_ref[:, :128] = (a[:, :128] * scale).astype(BF)
    o_ref[:, 128:] = (a[:, 128:] * scale).astype(BF)
    loop(PARTS, lambda d: lcopy(d, my).wait_send())


def detect(gs, ts, traces, templates):
    smem = pl.BlockSpec(memory_space=pltpu.SMEM)
    vmem = pl.BlockSpec(memory_space=pltpu.VMEM)
    hbm = pl.BlockSpec(memory_space=pltpu.HBM)
    dma = pltpu.SemaphoreType.DMA
    return pl.pallas_call(
        main_kernel,
        out_shape=jax.ShapeDtypeStruct((256, 256), BF),
        in_specs=[smem, vmem, vmem, hbm, hbm],
        out_specs=vmem,
        scratch_shapes=[
            pltpu.VMEM((NV, 256, 768), BF),
            pltpu.VMEM((NV, 6, 32, 128), BF),
            pltpu.VMEM((NV, 6, 32, 128), BF),
            pltpu.VMEM((NROW, 768), BF),
            pltpu.VMEM((16, 6, 24, 128), F32),
            pltpu.VMEM((2, 8, TPL, 128), BF),
            pltpu.VMEM((128, 2048), BF),
            pltpu.VMEM((768, 2048), BF),
            pltpu.VMEM((768, 2048), BF),
            pltpu.VMEM((8, TPL, 128), F32),
            pltpu.VMEM((PARTS, 4, 9600), BF),
            pltpu.VMEM((TPL, 9600), F32),
            pltpu.VMEM((TPL, 9600), BF),
            pltpu.VMEM((24, TPL, 512), BF),
            pltpu.VMEM((CHANS, STA, 2048), BF),
            pltpu.VMEM((CHANS, 1024, 128), F32),
            pltpu.VMEM((HOMES, 128), F32),
            pltpu.VMEM((HOMES, 2, 2, CHANS, 8, 128), BF),
            pltpu.VMEM((HOMES, 1, 128), F32),
            pltpu.VMEM((256, 256), F32),
            pltpu.VMEM((HOMES, 2, CHANS, 8, 128), BF),
            pltpu.VMEM((HOMES, 2, CHANS, 8, 128), BF),
            pltpu.VMEM((MEMBERS, CHANS, 8, 128), BF),
            pltpu.VMEM((MEMBERS, CHANS, 8, 128), BF),
            pltpu.VMEM((PARTS, HOMES, 1, 128), F32),
            pltpu.VMEM((HOMES, 128), F32),
            pltpu.VMEM((6, HOMES, 128), F32),
            pltpu.VMEM((8, 128), F32),
            pltpu.VMEM((PARTS, 8, 128), F32),
            dma((2,)),
            dma((PARTS,)), dma((PARTS,)),
            dma((HOMES,)), dma((HOMES,)),
            dma((2, HOMES)), dma((2, HOMES)),
            dma((PARTS,)), dma((PARTS,)),
            dma, dma,
            dma((PARTS,)), dma((PARTS,)),
        ],
        compiler_params=pltpu.CompilerParams(
            vmem_limit_bytes=56 << 20, collective_id=0, has_side_effects=True
        ),
    )(gs, gs, ts, traces, templates)


def body(traces, group_stations, template_stations, templates):
    o = detect(group_stations, template_stations.T, traces.transpose(1, 0, 2), templates)
    return o.reshape(16, 16, 8, TPL).transpose(3, 1, 0, 2).reshape(TPL, traces.shape[2])


def solution(mesh):
    placed = (P("tmpl", None, "tm"), P(), P("tmpl", None), P(("tmpl", "tm"), None))
    return jax.shard_map(
        body, mesh=mesh, in_specs=placed, out_specs=P("tmpl", "tm"), check_vma=False
    )
```

```python
import jax
import jax.numpy as jnp
from jax import lax
from jax.experimental import pallas as pl
from jax.experimental.pallas import tpu as pltpu
from jax.sharding import PartitionSpec as P

BF = jnp.bfloat16
F32 = jnp.float32
MESH = pl.DeviceIdType.MESH
HOMES, PARTS, STA, MEMBERS, TPL, CHANS = 32, 8, 64, 32, 32, 3
SAMPLES = 16384
NV = 51
NROW = 67 * 16
VU = 3
VD = 17


def lroll(x, s):
    s %= 128
    return x if s == 0 else pltpu.roll(x, s, 1)


def lane_bits(rows):
    lane = lax.broadcasted_iota(jnp.int32, (rows, 128), 1)
    return [((lane >> (3 + s)) & 1).astype(F32).astype(BF) > BF(0.5) for s in range(4)]


def swap_blocks(x, bits):
    x = list(x)
    for s in range(4):
        d = 1 << s
        y = list(x)
        for i in range(16):
            if i & d:
                continue
            a, b = x[i], x[i + d]
            if d == 8:
                turned = lroll(jnp.where(bits[s], a, b), 64)
                y[i] = jnp.where(bits[s], turned, a)
                y[i + d] = jnp.where(bits[s], b, turned)
            else:
                y[i] = jnp.where(bits[s], lroll(b, 8 * d), a)
                y[i + d] = jnp.where(bits[s], b, lroll(a, -8 * d))
        x = y
    return x


def main_kernel(
    gs_hbm, ts_hbm, tr_hbm, tp_hbm, o_ref, gs_ref, gv_ref, ts_ref,
    w_ref, w0_ref, p8_ref, e_ref, yf_ref, oh_ref, spread_ref, ta_ref, tb2_ref, tsb_ref, tg_ref, tf_ref, tb_ref, t_ref,
    tr_ref, rows_ref, pscr_ref, send_ref, pw_ref, acc_ref,
    r0_ref, r1_ref, hs_ref, hr_ref, pa_ref, p2_ref, inv_ref, ls_ref, la_ref,
    inload, tsend, trecv, psend, precv, xsend, xrecv, asend, arecv, hsend, hrecv, lsend, lrecv,
):
    me = lax.axis_index("tmpl")
    my = lax.axis_index("tm")
    rx = (r0_ref, r1_ref)
    twin = my + 1 - 2 * lax.rem(my, 2)

    def hop(d):
        i = lax.rem(8 - d % 8, 8)
        z = (i + 1) // 2 * (2 * (i % 2) - 1)
        return z, d // 8

    def home(d):
        z, x = hop(d)
        return lax.rem(me // 4 + 8 + z, 8) * 4 + lax.rem(me % 4 + x, 4)

    def part(d):
        return lax.rem(my + d, PARTS)

    def part_back(d):
        return lax.rem(my + PARTS - d, PARTS)

    def loop(n, f):
        def step(d, _):
            f(d)
            return 0

        lax.fori_loop(1, n, step, 0)

    def copy(src, dst, send, recv, to):
        return pltpu.make_async_remote_copy(
            src_ref=src, dst_ref=dst, send_sem=send, recv_sem=recv, device_id=to, device_id_type=MESH
        )

    def tcopy(d, slot):
        return copy(tg_ref.at[my], tg_ref.at[slot], tsend.at[d], trecv.at[slot], {"tm": part(2 * d)})

    def fcopy(d, slot):
        return copy(tg_ref.at[slot], tg_ref.at[slot], tsend.at[4 + d], trecv.at[slot], {"tm": twin})

    def pcopy(d, slot):
        to = home(d)
        return copy(pw_ref.at[to], pa_ref.at[my, slot], psend.at[d], precv, {"tmpl": to})

    def xcopy(d, half, slot):
        to = home(d)
        return copy(
            send_ref.at[to, half], rx[half].at[slot], xsend.at[half, d], xrecv.at[half], {"tmpl": to}
        )

    def rows_in(half):
        all_of = rx[half].at[pl.ds(0, HOMES - 1)]
        copy(all_of, all_of, xsend.at[half, 0], xrecv.at[half], {"tmpl": home(1)}).wait_recv()

    def powers_in():
        all_of = pa_ref.at[my, pl.ds(0, HOMES - 1)]
        copy(all_of, all_of, psend.at[0], precv, {"tmpl": home(1)}).wait_recv()

    def acopy(d, slot):
        return copy(pa_ref.at[my], pa_ref.at[slot], asend.at[d], arecv.at[slot], {"tm": part(d)})

    def hcopy():
        return copy(hs_ref, hr_ref, hsend, hrecv, {"tm": part(PARTS - 1)})

    def lcopy(d, slot):
        return copy(ls_ref, la_ref.at[slot], lsend.at[d], lrecv.at[slot], {"tm": part(d)})

    tin = pltpu.make_async_copy(tp_hbm, tg_ref.at[my], inload.at[0])
    xin = pltpu.make_async_copy(tr_hbm, tr_ref, inload.at[1])
    gin = pltpu.make_async_copy(gs_hbm, gv_ref, inload.at[2])
    sin = pltpu.make_async_copy(gs_hbm, gs_ref, inload.at[3])
    lin = pltpu.make_async_copy(ts_hbm, ts_ref, inload.at[4])
    xin.start()
    gin.start()
    tin.start()
    sin.start()
    lin.start()

    bar = pltpu.get_barrier_semaphore()
    loop(HOMES, lambda d: pl.semaphore_signal(bar, inc=1, device_id={"tmpl": home(d)}, device_id_type=MESH))
    loop(PARTS, lambda d: pl.semaphore_signal(bar, inc=1, device_id={"tm": part(d)}, device_id_type=MESH))

    gin.wait()
    local = (gv_ref[...] - me * STA).astype(F32)
    mine = (local >= 0) & (local < STA)
    low = jnp.min(jnp.where(mine, local, 1e6), axis=1, keepdims=True)
    high = jnp.max(jnp.where(mine, local, -1.0), axis=1, keepdims=True)
    high = jnp.where(high > low, high, -2.0)
    row = lax.broadcasted_iota(jnp.int32, (HOMES, STA), 1).astype(F32)
    pick = jnp.concatenate([(row == low).astype(F32), (row == high).astype(F32)], axis=0).astype(BF)
    lane = lax.broadcasted_iota(jnp.int32, (HOMES, 128), 1)
    power = jnp.zeros((HOMES, 128), F32)
    xin.wait()
    for c in range(CHANS):
        sq = jnp.zeros((64, 128), F32)
        for ch in range(4):
            res = jnp.dot(
                pick, tr_ref[c, :, ch * 512 : ch * 512 + 512], preferred_element_type=F32
            )
            for n in range(4):
                v = res[:, n * 128 : n * 128 + 128]
                sq = sq + v * v
                rows_ref[c, pl.ds(ch * 4 + n, 64, stride=16), :] = v
        tot = jnp.sum(sq, axis=1, keepdims=True)
        for i in range(2):
            power = jnp.where(lane == c * 2 + i, tot[i * 32 : i * 32 + 32], power)
    pscr_ref[...] = power

    def pack(g, _):
        for i in range(2):
            for c in range(CHANS):
                at = pl.ds(pl.multiple_of((i * 32 + g) * 16, 16), 16)
                v = rows_ref[c, at, :].astype(BF)
                send_ref[g, 0, i, c] = v[:8]
                send_ref[g, 1, i, c] = v[8:]
        pw_ref[g] = pscr_ref[pl.ds(g, 1), :]
        return 0

    lax.fori_loop(0, HOMES, pack, 0, unroll=4)
    tin.wait()
    sin.wait()
    lin.wait()
    pl.semaphore_wait(bar, HOMES + PARTS - 2)

    for d in range(1, 4):
        tcopy(d, my).start()
    fcopy(0, my).start()
    loop(HOMES, lambda d: xcopy(d, 0, me).start())
    loop(HOMES, lambda d: pcopy(d, me).start())
    loop(HOMES, lambda d: xcopy(d, 1, me).start())

    pa_ref[my, me] = pw_ref[me]
    for half in range(2):
        for i in range(2):
            for c in range(CHANS):
                rx[half][me, i, c] = send_ref[me, half, i, c]
    diag = lax.broadcasted_iota(jnp.int32, (TPL, TPL), 0) == lax.broadcasted_iota(
        jnp.int32, (TPL, TPL), 1
    )
    for s in range(8):
        ids = jnp.broadcast_to(ts_ref[s : s + 1, :], (TPL, TPL)).astype(F32)
        ids = jnp.sum(jnp.where(diag, ids, 0.0), axis=1, keepdims=True)
        tsb_ref[s] = jnp.broadcast_to(ids, (TPL, 128))

    block = lax.broadcasted_iota(jnp.int32, (TPL, 128), 1) >> 3
    for jh in range(2):
        ids = jnp.zeros((TPL, 128), F32)
        for jl in range(16):
            ids = jnp.where(block == jl, gs_ref[me, jh * 16 + jl].astype(F32), ids)
        for s in range(8):
            oh_ref[jh, s] = jnp.where(tsb_ref[s] == ids, 1.0, 0.0).astype(BF)
    row = lax.broadcasted_iota(jnp.int32, (128, 128), 0)
    lane = lax.broadcasted_iota(jnp.int32, (128, 128), 1) & 7
    for b in range(16):
        spread_ref[:, b * 128 : b * 128 + 128] = jnp.where(row == lane + 8 * b, 1.0, 0.0).astype(BF)

    for d in range(1, 4):
        tcopy(d, part_back(2 * d)).wait_recv()
        fcopy(d, part_back(2 * d)).start()
    for d in range(4):
        fcopy(d, lax.rem(twin + PARTS - 2 * d, PARTS)).wait_recv()

    def tstep(n, _):
        at = pl.ds(pl.multiple_of(n * 384, 128), 384)
        for b in range(PARTS):
            tf_ref[4 * b : 4 * b + 4, at] = tg_ref[b, :, at].astype(F32)
        tb_ref[:, at] = tf_ref[:, at].astype(BF)
        return 0

    lax.fori_loop(0, 25, tstep, 0)
    for n in range(24):
        t = tb_ref[:, n * 400 : n * 400 + 400]
        t_ref[n] = jnp.concatenate([t, jnp.zeros((TPL, 112), BF)], axis=1)

    w0_ref[NV - 1] = jnp.zeros_like(w0_ref[NV - 1])
    p8_ref[0] = jnp.zeros_like(p8_ref[0])

    def spread(t, to, blocks):
        for c in range(CHANS):
            x = [t_ref[s * CHANS + c, :, t * 128 : t * 128 + 128] for s in range(8)]
            x = jnp.concatenate(x, axis=0)
            x = jnp.dot(x, spread_ref[:, : blocks * 128], preferred_element_type=F32)
            to[c * 256 : c * 256 + 256, : blocks * 128] = x.astype(BF)

    def select(t, of, blocks):
        for kh in range(2):
            for jh in range(2):
                oh = [oh_ref[jh, s, kh * 16 : kh * 16 + 16, :] for s in range(8)]
                for b in range(blocks):
                    for c in range(CHANS):
                        pr = []
                        for s in range(8):
                            at = c * 256 + s * TPL + kh * 16
                            pr.append(oh[s] * of[at : at + 16, b * 128 : b * 128 + 128])
                        while len(pr) > 1:
                            pr = [pr[2 * n] + pr[2 * n + 1] for n in range(len(pr) // 2)]
                        w0_ref[16 * t + b, c * 2 + jh, kh * 16 : kh * 16 + 16, :] = pr[0]
                        p8_ref[16 * t + b + 1, c * 2 + jh, kh * 16 : kh * 16 + 16, :] = lroll(pr[0], -8)

    both = (ta_ref, tb2_ref)
    counts = (16, 16, 16, 2)
    spread(0, ta_ref, 16)
    for t in range(4):
        if t < 3:
            spread(t + 1, both[(t + 1) % 2], counts[t + 1])
        select(t, both[t % 2], counts[t])

    rows_in(0)

    def slot_of(j):
        h = gs_ref[me, j] // STA
        same = (j > 0) & (gs_ref[me, jnp.maximum(j - 1, 0)] // STA == h)
        return h, jnp.where(same, 1, 0)

    def hstep(j, _):
        h, i = slot_of(j)
        for c in range(CHANS):
            hs_ref[j, c] = r0_ref[h, i, c]
        return 0

    lax.fori_loop(0, MEMBERS, hstep, 0, unroll=4)
    hcopy().start()

    powers_in()
    loop(PARTS, lambda d: acopy(d, my).start())

    eighth = (lax.broadcasted_iota(jnp.int32, (32, 128), 1) & 7).astype(F32).astype(BF)

    def vstep(v, _):
        for r in range(8):
            keep = eighth < BF(8 - r) if r else None
            for u in range(VU):
                for g in range(6):
                    z = w0_ref[v * VU + u, g]
                    if r:
                        z = lroll(jnp.where(keep, z, p8_ref[v * VU + u, g]), r)
                    w_ref[v * VU + u, r * 32 : r * 32 + 32, g * 128 : g * 128 + 128] = z
        return 0

    lax.fori_loop(0, NV // VU, vstep, 0)

    loop(PARTS, lambda d: acopy(d, part_back(d)).wait_recv())
    for h in range(HOMES):
        s = pa_ref[0, h]
        for b in range(1, PARTS):
            s = s + pa_ref[b, h]
        p2_ref[h : h + 1, :] = s
    inv = 1.0 / jnp.sqrt(p2_ref[...] / SAMPLES + 1e-06)
    for n in range(6):
        inv_ref[n] = jnp.broadcast_to(inv[:, n : n + 1], (HOMES, 128))

    rows_in(1)
    hcopy().wait_recv()
    ahead = jnp.where(my < PARTS - 1, 1.0, 0.0)

    bits2 = lane_bits(48)

    def estep(c, _):
        tiles = []
        for jl in range(16):
            near, over = [], []
            for jh in range(2):
                j = jh * 16 + jl
                h, i = slot_of(j)
                at = inv_ref[c * 2 + i, pl.ds(h, 1), :]
                near.append(r0_ref[h, i, c].astype(F32) * at)
                near.append(r1_ref[h, i, c].astype(F32) * at)
                over.append(hr_ref[j, c].astype(F32) * (at * ahead))
            tiles.append(jnp.concatenate(near + over, axis=0).astype(BF))
        y = swap_blocks(tiles, bits2)
        for p in range(16):
            v = y[p].astype(F32)
            for jh in range(2):
                yf_ref[p, c * 2 + jh, 0:16, :] = v[16 * jh : 16 * jh + 16]
                yf_ref[p, c * 2 + jh, 16:24, :] = v[32 + 8 * jh : 40 + 8 * jh]
        return 0

    lax.fori_loop(0, CHANS, estep, 0)

    def pstep(p, _):
        for g in range(6):
            for m in range(4):
                at = pl.ds(pl.multiple_of((m * 16 + p) * 16, 16), 16)
                e_ref[at, g * 128 : g * 128 + 128] = yf_ref[p, g, m : m + 16, :].astype(BF)
        return 0

    lax.fori_loop(0, 16, pstep, 0)
    for p in range(3):
        for g in range(6):
            at = (64 + p) * 16
            e_ref[at : at + 16, g * 128 : g * 128 + 128] = yf_ref[p, g, 4:20, :].astype(BF)

    acc_ref[...] = jnp.zeros_like(acc_ref)

    def dstep(n, _):
        rows = [e_ref[pl.ds(pl.multiple_of((n * VD + i) * 16, 16), 256), :] for i in range(VD)]
        cols = [w_ref[n * VD + i] for i in range(VD)]
        acc_ref[...] += lax.dot_general(
            jnp.concatenate(rows, axis=1),
            jnp.concatenate(cols, axis=1),
            (((1,), (1,)), ((), ())),
            preferred_element_type=F32,
        )
        return 0

    lax.fori_loop(0, NV // VD, dstep, 0)

    a = acc_ref[...]
    s = jnp.sum(a * a, axis=0, keepdims=True)
    s = jnp.broadcast_to(s[:, :128] + s[:, 128:], (8, 128))
    s = s + lroll(s, 64)
    s = s + lroll(s, 32)
    ls_ref[...] = s
    la_ref[my] = s
    loop(PARTS, lambda d: lcopy(d, my).start())

    for d in range(1, 4):
        tcopy(d, my).wait_send()
    for d in range(4):
        fcopy(d, part_back(2 * d)).wait_send()
    loop(HOMES, lambda d: pcopy(d, me).wait_send())
    for half in range(2):
        loop(HOMES, lambda d: xcopy(d, half, me).wait_send())
    loop(PARTS, lambda d: acopy(d, my).wait_send())
    hcopy().wait_send()

    loop(PARTS, lambda d: lcopy(d, part_back(d)).wait_recv())
    level = la_ref[0]
    for b in range(1, PARTS):
        level = level + la_ref[b]
    scale = 1.0 / jnp.sqrt(level[0:1, :] / SAMPLES + 1e-06)
    a = acc_ref[...]
    o_ref[:, :128] = (a[:, :128] * scale).astype(BF)
    o_ref[:, 128:] = (a[:, 128:] * scale).astype(BF)
    loop(PARTS, lambda d: lcopy(d, my).wait_send())


def detect(gs, ts, traces, templates):
    vmem = pl.BlockSpec(memory_space=pltpu.VMEM)
    hbm = pl.BlockSpec(memory_space=pltpu.HBM)
    dma = pltpu.SemaphoreType.DMA
    return pl.pallas_call(
        main_kernel,
        out_shape=jax.ShapeDtypeStruct((256, 256), BF),
        in_specs=[hbm] * 4,
        out_specs=vmem,
        scratch_shapes=[
            pltpu.SMEM((MEMBERS, MEMBERS), jnp.int32),
            pltpu.VMEM((MEMBERS, MEMBERS), jnp.int32),
            pltpu.VMEM((8, TPL), jnp.int32),
            pltpu.VMEM((NV, 256, 768), BF),
            pltpu.VMEM((NV, 6, 32, 128), BF),
            pltpu.VMEM((NV, 6, 32, 128), BF),
            pltpu.VMEM((NROW, 768), BF),
            pltpu.VMEM((16, 6, 24, 128), F32),
            pltpu.VMEM((2, 8, TPL, 128), BF),
            pltpu.VMEM((128, 2048), BF),
            pltpu.VMEM((768, 2048), BF),
            pltpu.VMEM((768, 2048), BF),
            pltpu.VMEM((8, TPL, 128), F32),
            pltpu.VMEM((PARTS, 4, 9600), BF),
            pltpu.VMEM((TPL, 9600), F32),
            pltpu.VMEM((TPL, 9600), BF),
            pltpu.VMEM((24, TPL, 512), BF),
            pltpu.VMEM((CHANS, STA, 2048), BF),
            pltpu.VMEM((CHANS, 1024, 128), F32),
            pltpu.VMEM((HOMES, 128), F32),
            pltpu.VMEM((HOMES, 2, 2, CHANS, 8, 128), BF),
            pltpu.VMEM((HOMES, 1, 128), F32),
            pltpu.VMEM((256, 256), F32),
            pltpu.VMEM((HOMES, 2, CHANS, 8, 128), BF),
            pltpu.VMEM((HOMES, 2, CHANS, 8, 128), BF),
            pltpu.VMEM((MEMBERS, CHANS, 8, 128), BF),
            pltpu.VMEM((MEMBERS, CHANS, 8, 128), BF),
            pltpu.VMEM((PARTS, HOMES, 1, 128), F32),
            pltpu.VMEM((HOMES, 128), F32),
            pltpu.VMEM((6, HOMES, 128), F32),
            pltpu.VMEM((8, 128), F32),
            pltpu.VMEM((PARTS, 8, 128), F32),
            dma((5,)),
            dma((PARTS,)), dma((PARTS,)),
            dma((HOMES,)), dma,
            dma((2, HOMES)), dma((2,)),
            dma((PARTS,)), dma((PARTS,)),
            dma, dma,
            dma((PARTS,)), dma((PARTS,)),
        ],
        compiler_params=pltpu.CompilerParams(
            vmem_limit_bytes=56 << 20, collective_id=0, has_side_effects=True
        ),
    )(gs, ts, traces, templates)


def body(traces, group_stations, template_stations, templates):
    o = detect(group_stations, template_stations.T, traces.transpose(1, 0, 2), templates)
    return o.reshape(16, 16, 8, TPL).transpose(3, 1, 0, 2).reshape(TPL, traces.shape[2])


def solution(mesh):
    placed = (P("tmpl", None, "tm"), P(), P("tmpl", None), P(("tmpl", "tm"), None))
    return jax.shard_map(
        body, mesh=mesh, in_specs=placed, out_specs=P("tmpl", "tm"), check_vma=False
    )
```

```python
import jax
import jax.numpy as jnp
from jax import lax
from jax.experimental import pallas as pl
from jax.experimental.pallas import tpu as pltpu
from jax.sharding import PartitionSpec as P

BF = jnp.bfloat16
F32 = jnp.float32
MESH = pl.DeviceIdType.MESH
HOMES, PARTS, STA, MEMBERS, TPL, CHANS = 32, 8, 64, 32, 32, 3
SAMPLES = 16384
NV = 51
NROW = 67 * 16
VU = 3
VD = 17


def lroll(x, s):
    s %= 128
    return x if s == 0 else pltpu.roll(x, s, 1)


def lane_bits(rows):
    lane = lax.broadcasted_iota(jnp.int32, (rows, 128), 1)
    return [((lane >> (3 + s)) & 1).astype(F32).astype(BF) > BF(0.5) for s in range(4)]


def swap_blocks(x, bits):
    x = list(x)
    for s in range(4):
        d = 1 << s
        y = list(x)
        for i in range(16):
            if i & d:
                continue
            a, b = x[i], x[i + d]
            if d == 8:
                turned = lroll(jnp.where(bits[s], a, b), 64)
                y[i] = jnp.where(bits[s], turned, a)
                y[i + d] = jnp.where(bits[s], b, turned)
            else:
                y[i] = jnp.where(bits[s], lroll(b, 8 * d), a)
                y[i + d] = jnp.where(bits[s], b, lroll(a, -8 * d))
        x = y
    return x


def main_kernel(
    gs_hbm, ts_hbm, tr_hbm, tp_hbm, o_ref, gs_ref, gv_ref, ts_ref,
    w_ref, w0_ref, p8_ref, e_ref, yf_ref, turn_ref, oh_ref, spread_ref, ta_ref, tb2_ref, tsb_ref, tg_ref, tf_ref, tb_ref, t_ref,
    tr_ref, rows_ref, pscr_ref, send_ref, pw_ref, acc_ref,
    r0_ref, r1_ref, hs_ref, hr_ref, pa_ref, p2_ref, inv_ref, ls_ref, la_ref,
    inload, tsend, trecv, psend, precv, xsend, xrecv, asend, arecv, hsend, hrecv, lsend, lrecv,
):
    me = lax.axis_index("tmpl")
    my = lax.axis_index("tm")
    rx = (r0_ref, r1_ref)
    twin = my + 1 - 2 * lax.rem(my, 2)

    def hop(d):
        i = lax.rem(8 - d % 8, 8)
        z = (i + 1) // 2 * (2 * (i % 2) - 1)
        return z, d // 8

    def home(d):
        z, x = hop(d)
        return lax.rem(me // 4 + 8 + z, 8) * 4 + lax.rem(me % 4 + x, 4)

    def part(d):
        return lax.rem(my + d, PARTS)

    def part_back(d):
        return lax.rem(my + PARTS - d, PARTS)

    def loop(n, f):
        def step(d, _):
            f(d)
            return 0

        lax.fori_loop(1, n, step, 0)

    def copy(src, dst, send, recv, to):
        return pltpu.make_async_remote_copy(
            src_ref=src, dst_ref=dst, send_sem=send, recv_sem=recv, device_id=to, device_id_type=MESH
        )

    def tcopy(d, slot):
        return copy(tg_ref.at[my], tg_ref.at[slot], tsend.at[d], trecv.at[slot], {"tm": part(2 * d)})

    def fcopy(d, slot):
        return copy(tg_ref.at[slot], tg_ref.at[slot], tsend.at[4 + d], trecv.at[slot], {"tm": twin})

    def pcopy(d, slot):
        to = home(d)
        return copy(pw_ref.at[to], pa_ref.at[my, slot], psend.at[d], precv, {"tmpl": to})

    def xcopy(d, half, slot):
        to = home(d)
        return copy(
            send_ref.at[to, half], rx[half].at[slot], xsend.at[half, d], xrecv.at[half], {"tmpl": to}
        )

    def rows_in(half):
        all_of = rx[half].at[pl.ds(0, HOMES - 1)]
        copy(all_of, all_of, xsend.at[half, 0], xrecv.at[half], {"tmpl": home(1)}).wait_recv()

    def powers_in():
        all_of = pa_ref.at[my, pl.ds(0, HOMES - 1)]
        copy(all_of, all_of, psend.at[0], precv, {"tmpl": home(1)}).wait_recv()

    def acopy(d, slot):
        return copy(pa_ref.at[my], pa_ref.at[slot], asend.at[d], arecv.at[slot], {"tm": part(d)})

    def hcopy():
        return copy(hs_ref, hr_ref, hsend, hrecv, {"tm": part(PARTS - 1)})

    def lcopy(d, slot):
        return copy(ls_ref, la_ref.at[slot], lsend.at[d], lrecv.at[slot], {"tm": part(d)})

    tin = pltpu.make_async_copy(tp_hbm, tg_ref.at[my], inload.at[0])
    xin = pltpu.make_async_copy(tr_hbm, tr_ref, inload.at[1])
    gin = pltpu.make_async_copy(gs_hbm, gv_ref, inload.at[2])
    sin = pltpu.make_async_copy(gs_hbm, gs_ref, inload.at[3])
    lin = pltpu.make_async_copy(ts_hbm, ts_ref, inload.at[4])
    xin.start()
    gin.start()
    tin.start()
    sin.start()
    lin.start()

    bar = pltpu.get_barrier_semaphore()
    loop(HOMES, lambda d: pl.semaphore_signal(bar, inc=1, device_id={"tmpl": home(d)}, device_id_type=MESH))
    loop(PARTS, lambda d: pl.semaphore_signal(bar, inc=1, device_id={"tm": part(d)}, device_id_type=MESH))

    gin.wait()
    local = (gv_ref[...] - me * STA).astype(F32)
    mine = (local >= 0) & (local < STA)
    low = jnp.min(jnp.where(mine, local, 1e6), axis=1, keepdims=True)
    high = jnp.max(jnp.where(mine, local, -1.0), axis=1, keepdims=True)
    high = jnp.where(high > low, high, -2.0)
    row = lax.broadcasted_iota(jnp.int32, (HOMES, STA), 1).astype(F32)
    pick = jnp.concatenate([(row == low).astype(F32), (row == high).astype(F32)], axis=0).astype(BF)
    lane = lax.broadcasted_iota(jnp.int32, (HOMES, 128), 1)
    power = jnp.zeros((HOMES, 128), F32)
    xin.wait()
    for c in range(CHANS):
        sq = jnp.zeros((64, 128), F32)
        for ch in range(4):
            res = jnp.dot(
                pick, tr_ref[c, :, ch * 512 : ch * 512 + 512], preferred_element_type=F32
            )
            for n in range(4):
                v = res[:, n * 128 : n * 128 + 128]
                sq = sq + v * v
                rows_ref[c, pl.ds(ch * 4 + n, 64, stride=16), :] = v
        tot = jnp.sum(sq, axis=1, keepdims=True)
        for i in range(2):
            power = jnp.where(lane == c * 2 + i, tot[i * 32 : i * 32 + 32], power)
    pscr_ref[...] = power

    def pack(g, _):
        for i in range(2):
            for c in range(CHANS):
                at = pl.ds(pl.multiple_of((i * 32 + g) * 16, 16), 16)
                v = rows_ref[c, at, :].astype(BF)
                send_ref[g, 0, i, c] = v[:8]
                send_ref[g, 1, i, c] = v[8:]
        pw_ref[g] = pscr_ref[pl.ds(g, 1), :]
        return 0

    lax.fori_loop(0, HOMES, pack, 0, unroll=4)
    tin.wait()
    sin.wait()
    lin.wait()
    pl.semaphore_wait(bar, HOMES + PARTS - 2)

    for d in range(1, 4):
        tcopy(d, my).start()
    fcopy(0, my).start()
    loop(HOMES, lambda d: xcopy(d, 0, me).start())
    loop(HOMES, lambda d: pcopy(d, me).start())
    loop(HOMES, lambda d: xcopy(d, 1, me).start())

    pa_ref[my, me] = pw_ref[me]
    for half in range(2):
        for i in range(2):
            for c in range(CHANS):
                rx[half][me, i, c] = send_ref[me, half, i, c]
    diag = lax.broadcasted_iota(jnp.int32, (TPL, TPL), 0) == lax.broadcasted_iota(
        jnp.int32, (TPL, TPL), 1
    )
    for s in range(8):
        ids = jnp.broadcast_to(ts_ref[s : s + 1, :], (TPL, TPL)).astype(F32)
        ids = jnp.sum(jnp.where(diag, ids, 0.0), axis=1, keepdims=True)
        tsb_ref[s] = jnp.broadcast_to(ids, (TPL, 128))

    block = lax.broadcasted_iota(jnp.int32, (TPL, 128), 1) >> 3
    for jh in range(2):
        ids = jnp.zeros((TPL, 128), F32)
        for jl in range(16):
            ids = jnp.where(block == jl, gs_ref[me, jh * 16 + jl].astype(F32), ids)
        for s in range(8):
            oh_ref[jh, s] = jnp.where(tsb_ref[s] == ids, 1.0, 0.0).astype(BF)
    row = lax.broadcasted_iota(jnp.int32, (256, 256), 0)
    col = lax.broadcasted_iota(jnp.int32, (256, 256), 1)
    swap = ((row >> 4) == (col & 15)) & ((row & 15) == (col >> 4))
    weave = ((row >> 5) == (col & 7)) & ((row & 31) == (col >> 3))
    for n, one in enumerate((swap, weave)):
        one = jnp.where(one, 1.0, 0.0).astype(BF)
        for m in range(3):
            turn_ref[n, m * 256 : m * 256 + 256, :] = one
    row = lax.broadcasted_iota(jnp.int32, (128, 128), 0)
    lane = lax.broadcasted_iota(jnp.int32, (128, 128), 1) & 7
    for b in range(16):
        spread_ref[:, b * 128 : b * 128 + 128] = jnp.where(row == lane + 8 * b, 1.0, 0.0).astype(BF)

    for d in range(1, 4):
        tcopy(d, part_back(2 * d)).wait_recv()
        fcopy(d, part_back(2 * d)).start()
    for d in range(4):
        fcopy(d, lax.rem(twin + PARTS - 2 * d, PARTS)).wait_recv()

    def tstep(n, _):
        at = pl.ds(pl.multiple_of(n * 384, 128), 384)
        for b in range(PARTS):
            tf_ref[4 * b : 4 * b + 4, at] = tg_ref[b, :, at].astype(F32)
        tb_ref[:, at] = tf_ref[:, at].astype(BF)
        return 0

    lax.fori_loop(0, 25, tstep, 0)
    for n in range(24):
        t = tb_ref[:, n * 400 : n * 400 + 400]
        t_ref[n] = jnp.concatenate([t, jnp.zeros((TPL, 112), BF)], axis=1)

    w0_ref[NV - 1] = jnp.zeros_like(w0_ref[NV - 1])
    p8_ref[0] = jnp.zeros_like(p8_ref[0])

    def spread(t, to, blocks):
        for c in range(CHANS):
            x = [t_ref[s * CHANS + c, :, t * 128 : t * 128 + 128] for s in range(8)]
            x = jnp.concatenate(x, axis=0)
            x = jnp.dot(x, spread_ref[:, : blocks * 128], preferred_element_type=F32)
            to[c * 256 : c * 256 + 256, : blocks * 128] = x.astype(BF)

    def select(t, of, blocks):
        for kh in range(2):
            for jh in range(2):
                oh = [oh_ref[jh, s, kh * 16 : kh * 16 + 16, :] for s in range(8)]
                for b in range(blocks):
                    for c in range(CHANS):
                        pr = []
                        for s in range(8):
                            at = c * 256 + s * TPL + kh * 16
                            pr.append(oh[s] * of[at : at + 16, b * 128 : b * 128 + 128])
                        while len(pr) > 1:
                            pr = [pr[2 * n] + pr[2 * n + 1] for n in range(len(pr) // 2)]
                        w0_ref[16 * t + b, c * 2 + jh, kh * 16 : kh * 16 + 16, :] = pr[0]
                        p8_ref[16 * t + b + 1, c * 2 + jh, kh * 16 : kh * 16 + 16, :] = lroll(pr[0], -8)

    both = (ta_ref, tb2_ref)
    counts = (16, 16, 16, 2)
    spread(0, ta_ref, 16)
    for t in range(4):
        if t < 3:
            spread(t + 1, both[(t + 1) % 2], counts[t + 1])
        select(t, both[t % 2], counts[t])

    rows_in(0)

    def slot_of(j):
        h = gs_ref[me, j] // STA
        same = (j > 0) & (gs_ref[me, jnp.maximum(j - 1, 0)] // STA == h)
        return h, jnp.where(same, 1, 0)

    def hstep(j, _):
        h, i = slot_of(j)
        for c in range(CHANS):
            hs_ref[j, c] = r0_ref[h, i, c]
        return 0

    lax.fori_loop(0, MEMBERS, hstep, 0, unroll=4)
    hcopy().start()

    powers_in()
    loop(PARTS, lambda d: acopy(d, my).start())

    eighth = (lax.broadcasted_iota(jnp.int32, (32, 128), 1) & 7).astype(F32).astype(BF)

    def vstep(v, _):
        for r in range(8):
            keep = eighth < BF(8 - r) if r else None
            for u in range(VU):
                for g in range(6):
                    z = w0_ref[v * VU + u, g]
                    if r:
                        z = lroll(jnp.where(keep, z, p8_ref[v * VU + u, g]), r)
                    w_ref[v * VU + u, r * 32 : r * 32 + 32, g * 128 : g * 128 + 128] = z
        return 0

    lax.fori_loop(0, NV // VU, vstep, 0)

    loop(PARTS, lambda d: acopy(d, part_back(d)).wait_recv())
    for h in range(HOMES):
        s = pa_ref[0, h]
        for b in range(1, PARTS):
            s = s + pa_ref[b, h]
        p2_ref[h : h + 1, :] = s
    inv = 1.0 / jnp.sqrt(p2_ref[...] / SAMPLES + 1e-06)
    for n in range(6):
        inv_ref[n] = jnp.broadcast_to(inv[:, n : n + 1], (HOMES, 128))

    rows_in(1)
    hcopy().wait_recv()
    ahead = jnp.where(my < PARTS - 1, 1.0, 0.0)

    bits2 = lane_bits(48)

    def estep(c, _):
        tiles = []
        for jl in range(16):
            near, over = [], []
            for jh in range(2):
                j = jh * 16 + jl
                h, i = slot_of(j)
                at = inv_ref[c * 2 + i, pl.ds(h, 1), :]
                near.append(r0_ref[h, i, c].astype(F32) * at)
                near.append(r1_ref[h, i, c].astype(F32) * at)
                over.append(hr_ref[j, c].astype(F32) * (at * ahead))
            tiles.append(jnp.concatenate(near + over, axis=0).astype(BF))
        y = swap_blocks(tiles, bits2)
        for p in range(16):
            v = y[p].astype(F32)
            for jh in range(2):
                yf_ref[p, c * 2 + jh, 0:16, :] = v[16 * jh : 16 * jh + 16]
                yf_ref[p, c * 2 + jh, 16:24, :] = v[32 + 8 * jh : 40 + 8 * jh]
        return 0

    lax.fori_loop(0, CHANS, estep, 0)

    def pstep(p, _):
        for g in range(6):
            for m in range(4):
                at = pl.ds(pl.multiple_of((m * 16 + p) * 16, 16), 16)
                e_ref[at, g * 128 : g * 128 + 128] = yf_ref[p, g, m : m + 16, :].astype(BF)
        return 0

    lax.fori_loop(0, 16, pstep, 0)
    for p in range(3):
        for g in range(6):
            at = (64 + p) * 16
            e_ref[at : at + 16, g * 128 : g * 128 + 128] = yf_ref[p, g, 4:20, :].astype(BF)

    acc_ref[...] = jnp.zeros_like(acc_ref)

    def dstep(n, _):
        rows = [e_ref[pl.ds(pl.multiple_of((n * VD + i) * 16, 16), 256), :] for i in range(VD)]
        cols = [w_ref[n * VD + i] for i in range(VD)]
        acc_ref[...] += lax.dot_general(
            jnp.concatenate(cols, axis=1),
            jnp.concatenate(rows, axis=1),
            (((1,), (1,)), ((), ())),
            preferred_element_type=F32,
        )
        return 0

    lax.fori_loop(0, NV // VD, dstep, 0)

    a = acc_ref[...]
    s = jnp.sum(a * a, axis=1, keepdims=True)
    k = s[0:TPL]
    for r in range(1, 8):
        k = k + s[r * TPL : r * TPL + TPL]
    corner = lax.broadcasted_iota(jnp.int32, (TPL, 128), 0) == lax.broadcasted_iota(
        jnp.int32, (TPL, 128), 1
    )
    s = jnp.where(corner, jnp.broadcast_to(k, (TPL, 128)), 0.0)
    s = jnp.broadcast_to(jnp.sum(s, axis=0, keepdims=True), (8, 128))
    ls_ref[...] = s
    la_ref[my] = s
    loop(PARTS, lambda d: lcopy(d, my).start())

    def parts(x):
        one = x.astype(BF)
        rest = x - one.astype(F32)
        two = rest.astype(BF)
        three = (rest - two.astype(F32)).astype(BF)
        return jnp.concatenate([one, two, three], axis=1)

    z = jnp.dot(parts(a), turn_ref[0], preferred_element_type=F32)
    bands = []
    for h in range(8):
        cut = [z[r * 32 : r * 32 + 32, h * 32 : h * 32 + 32] for r in range(8)]
        bands.append(jnp.concatenate(cut, axis=1))
    z = jnp.concatenate(bands, axis=0)
    acc_ref[...] = jnp.dot(parts(z), turn_ref[1], preferred_element_type=F32)

    for d in range(1, 4):
        tcopy(d, my).wait_send()
    for d in range(4):
        fcopy(d, part_back(2 * d)).wait_send()
    loop(HOMES, lambda d: pcopy(d, me).wait_send())
    for half in range(2):
        loop(HOMES, lambda d: xcopy(d, half, me).wait_send())
    loop(PARTS, lambda d: acopy(d, my).wait_send())
    hcopy().wait_send()

    loop(PARTS, lambda d: lcopy(d, part_back(d)).wait_recv())
    level = la_ref[0]
    for b in range(1, PARTS):
        level = level + la_ref[b]
    level = jnp.where(corner, jnp.broadcast_to(level[0:1, :], (TPL, 128)), 0.0)
    scale = 1.0 / jnp.sqrt(jnp.sum(level, axis=1, keepdims=True) / SAMPLES + 1e-06)
    for h in range(8):
        o_ref[:, h * 256 : h * 256 + 256] = (acc_ref[h * 32 : h * 32 + 32, :] * scale).astype(BF)
    loop(PARTS, lambda d: lcopy(d, my).wait_send())


def detect(gs, ts, traces, templates):
    vmem = pl.BlockSpec(memory_space=pltpu.VMEM)
    hbm = pl.BlockSpec(memory_space=pltpu.HBM)
    dma = pltpu.SemaphoreType.DMA
    return pl.pallas_call(
        main_kernel,
        out_shape=jax.ShapeDtypeStruct((TPL, 2048), BF),
        in_specs=[hbm] * 4,
        out_specs=vmem,
        scratch_shapes=[
            pltpu.SMEM((MEMBERS, MEMBERS), jnp.int32),
            pltpu.VMEM((MEMBERS, MEMBERS), jnp.int32),
            pltpu.VMEM((8, TPL), jnp.int32),
            pltpu.VMEM((NV, 256, 768), BF),
            pltpu.VMEM((NV, 6, 32, 128), BF),
            pltpu.VMEM((NV, 6, 32, 128), BF),
            pltpu.VMEM((NROW, 768), BF),
            pltpu.VMEM((16, 6, 24, 128), F32),
            pltpu.VMEM((2, 768, 256), BF),
            pltpu.VMEM((2, 8, TPL, 128), BF),
            pltpu.VMEM((128, 2048), BF),
            pltpu.VMEM((768, 2048), BF),
            pltpu.VMEM((768, 2048), BF),
            pltpu.VMEM((8, TPL, 128), F32),
            pltpu.VMEM((PARTS, 4, 9600), BF),
            pltpu.VMEM((TPL, 9600), F32),
            pltpu.VMEM((TPL, 9600), BF),
            pltpu.VMEM((24, TPL, 512), BF),
            pltpu.VMEM((CHANS, STA, 2048), BF),
            pltpu.VMEM((CHANS, 1024, 128), F32),
            pltpu.VMEM((HOMES, 128), F32),
            pltpu.VMEM((HOMES, 2, 2, CHANS, 8, 128), BF),
            pltpu.VMEM((HOMES, 1, 128), F32),
            pltpu.VMEM((256, 256), F32),
            pltpu.VMEM((HOMES, 2, CHANS, 8, 128), BF),
            pltpu.VMEM((HOMES, 2, CHANS, 8, 128), BF),
            pltpu.VMEM((MEMBERS, CHANS, 8, 128), BF),
            pltpu.VMEM((MEMBERS, CHANS, 8, 128), BF),
            pltpu.VMEM((PARTS, HOMES, 1, 128), F32),
            pltpu.VMEM((HOMES, 128), F32),
            pltpu.VMEM((6, HOMES, 128), F32),
            pltpu.VMEM((8, 128), F32),
            pltpu.VMEM((PARTS, 8, 128), F32),
            dma((5,)),
            dma((PARTS,)), dma((PARTS,)),
            dma((HOMES,)), dma,
            dma((2, HOMES)), dma((2,)),
            dma((PARTS,)), dma((PARTS,)),
            dma, dma,
            dma((PARTS,)), dma((PARTS,)),
        ],
        compiler_params=pltpu.CompilerParams(
            vmem_limit_bytes=56 << 20, collective_id=0, has_side_effects=True
        ),
    )(gs, ts, traces, templates)


def body(traces, group_stations, template_stations, templates):
    return detect(group_stations, template_stations.T, traces.transpose(1, 0, 2), templates)


def solution(mesh):
    placed = (P("tmpl", None, "tm"), P(), P("tmpl", None), P(("tmpl", "tm"), None))
    return jax.shard_map(
        body, mesh=mesh, in_specs=placed, out_specs=P("tmpl", "tm"), check_vma=False
    )
```
